32 devices in a mesh: grp: 2 (over x), tm: 16 (over z, y, core).
Axes of the slice: x: 2, y: 2, z: 4, core: 2. Of those that a mesh axis runs over, the one named last changes fastest.
Arguments:
- noise: float32 [32, 256, 256], P(('grp', 'tm')), parts along dimension 0, may hold values from -6 to 6
- phonon_level: int32 [32, 256, 256], P(('grp', 'tm')), parts along dimension 0, may hold values from 0 to 16
- hop_x: float32 [256, 256], replicated, as said below
- hop_y: float32 [256, 256], replicated, as said below
Outputs:
- solution: float32 [32, 256, 256], P(('grp', 'tm')), parts along dimension 0
- residual: float32 [32, 256, 256], P(('grp', 'tm')), parts along dimension 0
The draws below stay inside these ranges and needn't reach their ends.
There are 2 independent parts, one for each index of `grp`. The reference program is written for one: setup_inputs(seed, part) draws one part's arguments, and reference() takes and returns one part's arrays. A program takes and returns all parts, laid end to end along the dimension named above; an argument that names none is the same for every part. Nothing has to cross between parts.
Inputs may be any that keep to these rules, and one draw needn't show every extreme that they name: hop_x is symmetric. hop_y is symmetric.
All inputs are finite; a program needn't handle non-finite values.
Results may differ from the reference program's by a relative error of at most 0.0003.
Values sent between devices are 32-bit elements; how exact they have to be, the bound alone decides.
No kernel may reach another device: no remote copies, remote signals or barrier semaphores. Data moves between devices by JAX's collectives and lax.ppermute only.
A program may use at most 64 MiB of HBM per device.

```python
import math
import jax
import jax.numpy as jnp
from jax import lax

LX = 256
LY = 256
ORDER = 10
LEVELS = 17
L = 16


def draw_phonon_level(key, part):
    times = jnp.arange(L, dtype=jnp.int32)
    offset = (LEVELS - 9) * times // (L - 1)
    levels = jax.random.randint(key, (L, LX, LY), 0, 9, dtype=jnp.int32) + offset[:, None, None]
    levels = levels.at[0, 0, 0].set(0)
    levels = levels.at[L - 1, 0, 0].set(LEVELS - 1)
    return levels


def hop_matrix(key, length):
    noise_part = jax.random.normal(key, (length, length), jnp.float32)
    noise_part = noise_part * (0.25 / math.sqrt(length))
    return jnp.eye(length, dtype=jnp.float32) + (noise_part + noise_part.T) * 0.70710678


def draw_hop_x(key, part):
    return hop_matrix(jax.random.fold_in(key, 11), LX)


def draw_hop_y(key, part):
    return hop_matrix(jax.random.fold_in(key, 12), LY)


def block_levels(own_key, shape, split, smallest, largest):
    def one(dim, blocks):
        steps = jax.random.uniform(jax.random.fold_in(jax.random.fold_in(own_key, 6), dim), (blocks,), jnp.float32, smallest / len(split), largest / len(split))
        return jnp.repeat(jnp.exp(steps), shape[dim] // blocks).reshape((-1,) + (1,) * (len(shape) - dim - 1))

    loudness = one(*split[0])
    for cut in split[1:]:
        loudness = loudness * one(*cut)
    return loudness


def bell_draw(key, shape, scale, bound, shards=(), kind=jnp.bfloat16):
    loudness = block_levels(key, shape, shards, -0.22, 0.18) if shards else 1.0
    values = jax.random.normal(key, shape, jnp.float32) * scale * loudness
    return jnp.minimum(jnp.maximum(values, -bound), bound).astype(kind)


def setup_inputs(seed: int = 0, part: int = 0) -> dict:
    splits = jax.random.split(jax.random.key(seed), 5)
    own_keys = jax.random.split(jax.random.fold_in(splits[4], part), 5)
    noise = bell_draw(own_keys[0], (L, LX, LY), 1.0, 6.0, ((0, 16),), jnp.float32)
    phonon_level = draw_phonon_level(jax.random.fold_in(jax.random.fold_in(splits[4], part), 71), part)
    hop_x = draw_hop_x(jax.random.fold_in(splits[4], 71), part)
    hop_y = draw_hop_y(jax.random.fold_in(splits[4], 71), part)
    return {"noise": noise, "phonon_level": phonon_level, "hop_x": hop_x, "hop_y": hop_y}


def propagate(field, hop_x, hop_y):
    inner = jnp.einsum('ax,nxy->nay', hop_x, field, precision=lax.Precision.HIGHEST)
    return jnp.einsum('nay,yb->nab', inner, hop_y, precision=lax.Precision.HIGHEST)

def normal_apply(vector, damp, hop_x, hop_y):
    length = vector.shape[0]
    positions = jnp.arange(length, dtype=jnp.int32)
    first_sign = jnp.where(positions == 0, -1.0, 1.0).astype(jnp.float32)[:, None, None]
    last_sign = jnp.where(positions == length - 1, -1.0, 1.0).astype(jnp.float32)[:, None, None]
    previous = jnp.roll(vector, 1, axis=0) * first_sign
    forward = vector - propagate(damp * previous, hop_x, hop_y)
    carried = damp * propagate(forward, hop_x, hop_y)
    following = jnp.roll(carried, -1, axis=0) * last_sign
    return forward - following

def chebyshev(field, cosines, cbar, hop_x, hop_y):
    lower_edge = 0.05
    upper_edge = (1.0 + 3.0 * cbar) ** 2
    center = (upper_edge + lower_edge) / (upper_edge - lower_edge)
    radius_term = jnp.sqrt(center * center - 1.0)
    ratio = center - radius_term
    cos_block = cosines[:, None, None]

    def apply_shifted(vector):
        once = propagate(vector, hop_x, hop_y)
        twice = propagate(once, hop_x, hop_y)
        normal_part = vector + cbar * cbar * twice - 2.0 * cbar * cos_block * once
        return (2.0 * normal_part - (upper_edge + lower_edge) * vector) / (upper_edge - lower_edge)
    previous = field
    current = apply_shifted(field)
    weight = -ratio
    total_sum = previous + 2.0 * weight * current
    for degree in range(2, ORDER + 1):
        following = 2.0 * apply_shifted(current) - previous
        weight = weight * -ratio
        total_sum = total_sum + 2.0 * weight * following
        previous = current
        current = following
    return total_sum * (2.0 / ((upper_edge - lower_edge) * radius_term))

def precondition(resid, cbar, hop_x, hop_y):
    length = resid.shape[0]
    times = jnp.arange(length, dtype=jnp.int32)
    phase = (2 * times[:, None] + 1) * times[None, :] % (2 * length)
    angles = phase.astype(jnp.float32) * (math.pi / length)
    cos_table = jnp.cos(angles)
    sin_table = jnp.sin(angles)
    flat = resid.reshape(length, -1)
    real_part = jnp.dot(cos_table, flat, precision=lax.Precision.HIGHEST)
    imag_part = -jnp.dot(sin_table, flat, precision=lax.Precision.HIGHEST)
    cosines = jnp.cos((2 * times + 1).astype(jnp.float32) * (math.pi / length))
    stacked = jnp.concatenate([real_part, imag_part], axis=0).reshape(2 * length, resid.shape[1], resid.shape[2])
    result = chebyshev(stacked, jnp.concatenate([cosines, cosines]), cbar, hop_x, hop_y)
    result = result.reshape(2 * length, -1)
    back = jnp.dot(cos_table.T, result[:length], precision=lax.Precision.HIGHEST) - jnp.dot(sin_table.T, result[length:], precision=lax.Precision.HIGHEST)
    return (back / length).reshape(resid.shape)

def reference(noise, phonon_level, hop_x, hop_y):
    middle = (LEVELS - 1) // 2
    levels = phonon_level.astype(jnp.float32)
    damp = jnp.exp(-0.05 * (levels - middle))
    mean_level = jnp.sum(levels) / (L * LX * LY)
    cbar = jnp.exp(-0.05 * (mean_level - middle))
    first = precondition(noise, cbar, hop_x, hop_y)
    second_residual = noise - normal_apply(first, damp, hop_x, hop_y)
    solution = first + precondition(second_residual, cbar, hop_x, hop_y)
    residual = noise - normal_apply(solution, damp, hop_x, hop_y)
    return (solution, residual)
```

```python
import math

import jax
import jax.numpy as jnp
import numpy as np
from jax import lax
from jax.experimental import pallas as pl
from jax.experimental.pallas import tpu as pltpu
from jax.sharding import PartitionSpec as P

ORDER = 10
LEVELS = 17
MIDDLE = (LEVELS - 1) // 2
BF16 = jnp.bfloat16
F32 = jnp.float32
VMEM = pl.BlockSpec(memory_space=pltpu.VMEM)


def call(kernel, out_shape, count, scratch=()):
    return pl.pallas_call(
        kernel,
        out_shape=out_shape,
        in_specs=[VMEM] * count,
        out_specs=jax.tree.map(lambda _: VMEM, out_shape),
        scratch_shapes=list(scratch),
        compiler_params=pltpu.CompilerParams(vmem_limit_bytes=16 << 20),
    )


def shape(rows, columns, kind=F32):
    return jax.ShapeDtypeStruct((rows, columns), kind)


def split(value):
    high = value.astype(BF16)
    return high, (value - high.astype(F32)).astype(BF16)


def dot3(left, right):
    def dot(a, b):
        return jnp.dot(a, b, preferred_element_type=F32)

    return dot(left[0], right[0]) + (dot(left[1], right[0]) + dot(left[0], right[1]))


def prepare_kernel(hop_x_ref, hop_y_ref, xh_ref, xl_ref, yh_ref, yl_ref):
    for ref, high_ref, low_ref in ((hop_x_ref, xh_ref, xl_ref), (hop_y_ref, yh_ref, yl_ref)):
        side = ref.shape[0]
        hop = ref[...]
        square = jnp.dot(hop, hop, precision=lax.Precision.HIGHEST, preferred_element_type=F32)
        high_ref[:side], low_ref[:side] = split(hop)
        high_ref[side:], low_ref[side:] = split(square)


def transform_kernel(block_ref, th_ref, tl_ref, out_ref):
    rows, columns = block_ref.shape
    block = split(block_ref[...])
    result = dot3((th_ref[...], tl_ref[...]), block)
    for part in range(th_ref.shape[0] // rows):
        out_ref[:, part * columns : (part + 1) * columns] = result[part * rows : (part + 1) * rows]


def chebyshev_kernel(*refs):
    field_ref, xh_ref, xl_ref, yh_ref, yl_ref, sum_ref, cos_ref = refs[:7]
    add_ref = refs[7] if len(refs) == 10 else None
    out_ref, weight_ref = refs[-2:]
    side_x = field_ref.shape[0]
    side_y = field_ref.shape[1]
    cbar = jnp.exp(-0.05 * (sum_ref[...] - MIDDLE))
    lower = 0.05
    root_lower = math.sqrt(lower)
    root_upper = 1.0 + 3.0 * cbar
    upper = root_upper * root_upper
    spread = upper - lower
    ratio = (root_upper - root_lower) / (root_upper + root_lower)
    keep = 2.0 * (2.0 - (upper + lower)) / spread
    once = -8.0 * cos_ref[...] * cbar / spread
    twice = 4.0 * cbar * cbar / spread
    weight = 2.0 / (root_upper * root_lower)
    for degree in range(ORDER + 1):
        weight_ref[degree : degree + 1, :] = weight
        weight = weight * -ratio
    field = field_ref[...]
    x_pair = (xh_ref[...], xl_ref[...])

    def step(index, carry):
        ahead, second = carry
        inner = dot3(x_pair, split(ahead))
        first_h, first_l = split(inner[:side_x] * once)
        second_h, second_l = split(inner[side_x:] * twice)
        hops = dot3((first_h, first_l), (yh_ref[:side_y], yl_ref[:side_y])) + dot3(
            (second_h, second_l), (yh_ref[side_y:], yl_ref[side_y:])
        )
        row = weight_ref[pl.ds(ORDER - 1 - index, 1), :]
        return (row * field + keep * ahead - second) + hops, ahead

    last = weight_ref[ORDER : ORDER + 1, :] * field
    ahead, before = last, last - last

    def body(index, carry):
        first, second, _ = carry
        result, first_out = step(index, (first, second))
        return result, first_out, second

    result, _, second = lax.fori_loop(0, ORDER, body, (ahead, before, before))
    total = 0.5 * (result - second)
    out_ref[...] = total if add_ref is None else total + add_ref[...]


def normal_kernel(
    even_ref, slices_ref, other_ref, damp_ref, damp_next_ref, noise_ref, xh_ref, xl_ref, yh_ref, yl_ref, out_ref
):
    side_x, side_y = other_ref.shape
    x_pair = (xh_ref[:side_x], xl_ref[:side_x])
    y_pair = (yh_ref[:side_y], yl_ref[:side_y])
    even = even_ref[...] > 0.5
    far = slices_ref[:, :side_y]
    here = slices_ref[:, side_y:]
    near = other_ref[...]
    before = jnp.where(even, far, near)
    after = jnp.where(even, near, far)
    damp_next = damp_next_ref[...]

    def propagate(value):
        return dot3(split(dot3(x_pair, split(value))), y_pair)

    forward = here - propagate(damp_ref[...] * before)
    forward_next = after - propagate(damp_next * here)
    out_ref[...] = noise_ref[...] - (forward - damp_next * propagate(forward_next))


def tables(length, rows):
    times = np.arange(length)
    phase = (2 * (times // 2)[:, None] + 1) * times[None, :] % (2 * length)
    angles = phase * (math.pi / length)
    basis = np.where((times % 2 == 0)[:, None], np.cos(angles), np.sin(angles))
    inverse = basis.T * (2.0 / length)
    far = np.where(times % 2 == 0, times - 1, times + 1)
    wrapped = np.where((far < 0) | (far >= length), -1.0, 1.0)
    inverse_far = inverse[far % length] * wrapped[:, None]

    def parts(matrix):
        matrix = np.kron(matrix, np.eye(rows))
        high = matrix.astype(BF16)
        return jnp.asarray(high), jnp.asarray((matrix - high.astype(np.float64)).astype(BF16))

    forward = parts(basis)
    back_far, back = parts(inverse_far), parts(inverse)
    both = tuple(jnp.concatenate([a, b], axis=0) for a, b in zip(back_far, back))
    return forward, both


def total_over(value, axis):
    count = lax.axis_size(axis)
    if count & (count - 1):
        return lax.psum(value, axis)
    step = 1
    while step < count:
        value = value + lax.ppermute(value, axis, [(i, i ^ step) for i in range(count)])
        step *= 2
    return value


def exchange(value, axis):
    count = lax.axis_size(axis)
    rows, columns = value.shape
    blocks = value.reshape(count, rows // count, columns)
    return lax.all_to_all(blocks, axis, split_axis=0, concat_axis=0, tiled=True).reshape(rows, columns)


def per_device(noise, phonon_level, hop_x, hop_y):
    _, side_x, side_y = noise.shape
    length = lax.axis_size("tm")
    position = lax.axis_index("tm")
    noise = noise[0]
    levels = phonon_level[0].astype(F32)
    damp = jnp.exp(-0.05 * (levels - MIDDLE))
    damp_next = lax.ppermute(damp, "tm", [(i, (i - 1) % length) for i in range(length)])
    level_sum = total_over(jnp.full((1, side_y), jnp.sum(levels), F32), "tm")
    mean_level = level_sum / (length * side_x * side_y)
    cosine = jnp.cos((2 * (position // 2) + 1).astype(F32) * (math.pi / length))
    cosine = jnp.full((1, side_y), cosine, F32)
    even = jnp.full((1, side_y), (position % 2 == 0).astype(F32), F32)
    forward, back = tables(length, side_x // length)

    hops = call(prepare_kernel, (shape(2 * side_x, side_x, BF16),) * 2 + (shape(2 * side_y, side_y, BF16),) * 2, 2)(
        hop_x, hop_y
    )
    field_shape = shape(side_x, side_y)
    to_spectrum = call(transform_kernel, field_shape, 3)
    to_times = call(transform_kernel, shape(side_x, 2 * side_y), 3)

    def chebyshev(*operands):
        return call(chebyshev_kernel, field_shape, len(operands), [pltpu.VMEM((16, side_y), F32)])(*operands)

    def spectrum(field):
        return exchange(to_spectrum(exchange(field, "tm"), *forward), "tm")

    def slices_of(components):
        slices = exchange(to_times(exchange(components, "tm"), *back), "tm")
        here = slices[:, side_y:]
        other = lax.ppermute(here, "tm", [(i, i ^ 1) for i in range(length)])
        return slices, here, other

    def residual_of(slices, other):
        return call(normal_kernel, field_shape, 10)(even, slices, other, damp, damp_next, noise, *hops)

    first = chebyshev(spectrum(noise), *hops, mean_level, cosine)
    slices, _, other = slices_of(first)
    second_residual = residual_of(slices, other)
    total = chebyshev(spectrum(second_residual), *hops, mean_level, cosine, first)
    slices, result, other = slices_of(total)
    residual = residual_of(slices, other)
    return result[None], residual[None]


def solution(mesh):
    return jax.shard_map(
        per_device,
        mesh=mesh,
        in_specs=(P(("grp", "tm"), None, None), P(("grp", "tm"), None, None), P(), P()),
        out_specs=(P(("grp", "tm"), None, None), P(("grp", "tm"), None, None)),
        check_vma=False,
    )
```

```python
import math

import jax
import jax.numpy as jnp
import numpy as np
from jax import lax
from jax.experimental import pallas as pl
from jax.experimental.pallas import tpu as pltpu
from jax.sharding import PartitionSpec as P

ORDER = 10
LEVELS = 17
MIDDLE = (LEVELS - 1) // 2
BF16 = jnp.bfloat16
F32 = jnp.float32
VMEM = pl.BlockSpec(memory_space=pltpu.VMEM)


def call(kernel, out_shape, count, scratch=(), passes=0):
    return pl.pallas_call(
        kernel,
        out_shape=out_shape,
        in_specs=[VMEM] * count,
        out_specs=jax.tree.map(lambda _: VMEM, out_shape),
        scratch_shapes=list(scratch),
        compiler_params=pltpu.CompilerParams(vmem_limit_bytes=16 << 20),
        cost_estimate=pl.CostEstimate(flops=passes, transcendentals=0, bytes_accessed=0) if passes else None,
    )


def shape(rows, columns, kind=F32):
    return jax.ShapeDtypeStruct((rows, columns), kind)


def split(value):
    high = value.astype(BF16)
    return high, (value - high.astype(F32)).astype(BF16)


def dot3(left, right):
    def dot(a, b):
        return jnp.dot(a, b, preferred_element_type=F32)

    return dot(left[0], right[0]) + (dot(left[1], right[0]) + dot(left[0], right[1]))


def prepare_kernel(hop_x_ref, hop_y_ref, xh_ref, xl_ref, yh_ref, yl_ref):
    for ref, high_ref, low_ref in ((hop_x_ref, xh_ref, xl_ref), (hop_y_ref, yh_ref, yl_ref)):
        side = ref.shape[0]
        hop = ref[...]
        square = jnp.dot(hop, hop, precision=lax.Precision.HIGHEST, preferred_element_type=F32)
        high_ref[:side], low_ref[:side] = split(hop)
        high_ref[side:], low_ref[side:] = split(square)


def transform_kernel(block_ref, th_ref, tl_ref, out_ref):
    rows, columns = block_ref.shape
    block = split(block_ref[...])
    result = dot3((th_ref[...], tl_ref[...]), block)
    for part in range(th_ref.shape[0] // rows):
        out_ref[:, part * columns : (part + 1) * columns] = result[part * rows : (part + 1) * rows]


def chebyshev_kernel(*refs):
    field_ref, xh_ref, xl_ref, yh_ref, yl_ref, sum_ref, cos_ref = refs[:7]
    add_ref = refs[7] if len(refs) == 10 else None
    out_ref, weight_ref = refs[-2:]
    side_x = field_ref.shape[0]
    side_y = field_ref.shape[1]
    mean_level = jnp.sum(sum_ref[...], axis=0, keepdims=True)
    cbar = jnp.exp(-0.05 * (mean_level - MIDDLE))
    lower = 0.05
    root_lower = math.sqrt(lower)
    root_upper = 1.0 + 3.0 * cbar
    upper = root_upper * root_upper
    spread = upper - lower
    ratio = (root_upper - root_lower) / (root_upper + root_lower)
    keep = 2.0 * (2.0 - (upper + lower)) / spread
    once = -8.0 * cos_ref[...] * cbar / spread
    twice = 4.0 * cbar * cbar / spread
    weight = 2.0 / (root_upper * root_lower)
    for degree in range(ORDER + 1):
        weight_ref[degree : degree + 1, :] = weight
        weight = weight * -ratio
    field = field_ref[...]
    half = side_x // 2

    def left(start, value):
        window = slice(start, start + half)
        return dot3((xh_ref[window], xl_ref[window]), value)

    def body(index, carry):
        ahead, second, _ = carry
        value = split(ahead)
        row = weight_ref[pl.ds(ORDER - 1 - index, 1), :]
        inner = [
            (split(left(start, value) * once), split(left(side_x + start, value) * twice)) for start in (0, half)
        ]
        parts = []
        for start, (single, double) in zip((0, half), inner):
            window = slice(start, start + half)
            hops = dot3(single, (yh_ref[:side_y], yl_ref[:side_y])) + dot3(double, (yh_ref[side_y:], yl_ref[side_y:]))
            parts.append((row * field[window] + keep * ahead[window] - second[window]) + hops)
        return jnp.concatenate(parts, axis=0), ahead, second

    ahead = weight_ref[ORDER : ORDER + 1, :] * field
    before = ahead - ahead
    result, _, second = lax.fori_loop(0, ORDER, body, (ahead, before, before), unroll=ORDER // 2)
    total = 0.5 * (result - second)
    out_ref[...] = total if add_ref is None else total + add_ref[...]


def normal_kernel(
    even_ref, slices_ref, other_ref, damp_ref, damp_next_ref, noise_ref, xh_ref, xl_ref, yh_ref, yl_ref, out_ref
):
    side_x, side_y = other_ref.shape
    half = side_x // 2
    windows = (slice(0, half), slice(half, side_x))
    y_pair = (yh_ref[:side_y], yl_ref[:side_y])
    even = even_ref[...] > 0.5
    far = slices_ref[:, :side_y]
    here = slices_ref[:, side_y:]
    near = other_ref[...]
    before = jnp.where(even, far, near)
    after = jnp.where(even, near, far)
    damp_next = damp_next_ref[...]

    def propagate(value):
        value = split(value)
        inner = [split(dot3((xh_ref[window], xl_ref[window]), value)) for window in windows]
        return [dot3(part, y_pair) for part in inner]

    moved = propagate(damp_next * here)
    forward_next = jnp.concatenate([after[window] - part for window, part in zip(windows, moved)], axis=0)
    moved = propagate(damp_ref[...] * before)
    carried = propagate(forward_next)
    for window, part, back in zip(windows, moved, carried):
        forward = here[window] - part
        out_ref[window] = noise_ref[window] - (forward - damp_next[window] * back)


def tables(length, rows):
    times = np.arange(length)
    phase = (2 * (times // 2)[:, None] + 1) * times[None, :] % (2 * length)
    angles = phase * (math.pi / length)
    basis = np.where((times % 2 == 0)[:, None], np.cos(angles), np.sin(angles))
    inverse = basis.T * (2.0 / length)
    far = np.where(times % 2 == 0, times - 1, times + 1)
    wrapped = np.where((far < 0) | (far >= length), -1.0, 1.0)
    inverse_far = inverse[far % length] * wrapped[:, None]

    def parts(matrix):
        matrix = np.kron(matrix, np.eye(rows))
        high = matrix.astype(BF16)
        return jnp.asarray(high), jnp.asarray((matrix - high.astype(np.float64)).astype(BF16))

    forward = parts(basis)
    back_far, back = parts(inverse_far), parts(inverse)
    both = tuple(jnp.concatenate([a, b], axis=0) for a, b in zip(back_far, back))
    return forward, both


def add_partners(value, axis, step):
    count = lax.axis_size(axis)
    value = jnp.sum(value, axis=0, keepdims=True)
    shifts = range(1, min(4, count // step))
    others = [lax.ppermute(value, axis, [(i, i ^ (step * shift)) for i in range(count)]) for shift in shifts]
    return jnp.concatenate([value] + others, axis=0)


def exchange(value, axis):
    count = lax.axis_size(axis)
    rows, columns = value.shape
    blocks = value.reshape(count, rows // count, columns)
    return lax.all_to_all(blocks, axis, split_axis=0, concat_axis=0, tiled=True).reshape(rows, columns)


def per_device(noise, phonon_level, hop_x, hop_y):
    _, side_x, side_y = noise.shape
    length = lax.axis_size("tm")
    position = lax.axis_index("tm")
    noise = noise[0]
    levels = phonon_level[0].astype(F32)
    damp = jnp.exp(-0.05 * (levels - MIDDLE))
    mean_rows = jnp.full((1, side_y), jnp.sum(levels) / (length * side_x * side_y), F32)
    cosine = jnp.cos((2 * (position // 2) + 1).astype(F32) * (math.pi / length))
    cosine = jnp.full((1, side_y), cosine, F32)
    even = jnp.full((1, side_y), (position % 2 == 0).astype(F32), F32)
    forward, back = tables(length, side_x // length)

    hops = call(prepare_kernel, (shape(2 * side_x, side_x, BF16),) * 2 + (shape(2 * side_y, side_y, BF16),) * 2, 2)(
        hop_x, hop_y
    )
    field_shape = shape(side_x, side_y)
    to_spectrum = call(transform_kernel, field_shape, 3)
    to_times = call(transform_kernel, shape(side_x, 2 * side_y), 3)

    work = 12 * ORDER * 2 * side_x * side_y * max(side_x, side_y)

    def chebyshev(*operands):
        return call(chebyshev_kernel, field_shape, len(operands), [pltpu.VMEM((16, side_y), F32)], work)(*operands)

    def spectrum(field, beside):
        block = to_spectrum(exchange(field, "tm"), *forward)
        block, beside = lax.optimization_barrier((block, beside))
        return exchange(block, "tm"), beside

    def slices_of(components):
        slices = exchange(to_times(exchange(components, "tm"), *back), "tm")
        here = slices[:, side_y:]
        other = lax.ppermute(here, "tm", [(i, i ^ 1) for i in range(length)])
        return slices, here, other

    def residual_of(slices, other):
        return call(normal_kernel, field_shape, 10)(even, slices, other, damp, damp_next, noise, *hops)

    power_of_two = length & (length - 1) == 0
    mean_rows = add_partners(mean_rows, "tm", 1) if power_of_two else lax.psum(mean_rows, "tm")
    field, mean_rows = spectrum(noise, mean_rows)
    step = 4
    while power_of_two and step < length:
        mean_rows = add_partners(mean_rows, "tm", step)
        step *= 4
    field, damp = lax.optimization_barrier((field, damp))
    damp_next = lax.ppermute(damp, "tm", [(i, (i - 1) % length) for i in range(length)])
    first = chebyshev(field, *hops, mean_rows, cosine)
    first, damp_next = lax.optimization_barrier((first, damp_next))

    slices, _, other = slices_of(first)
    second_residual = residual_of(slices, other)
    field, _ = spectrum(second_residual, cosine)
    total = chebyshev(field, *hops, mean_rows, cosine, first)
    slices, result, other = slices_of(total)
    residual = residual_of(slices, other)
    return result[None], residual[None]


def solution(mesh):
    return jax.shard_map(
        per_device,
        mesh=mesh,
        in_specs=(P(("grp", "tm"), None, None), P(("grp", "tm"), None, None), P(), P()),
        out_specs=(P(("grp", "tm"), None, None), P(("grp", "tm"), None, None)),
        check_vma=False,
    )
```

```python
import math

import jax
import jax.numpy as jnp
import numpy as np
from jax import lax
from jax.experimental import pallas as pl
from jax.experimental.pallas import tpu as pltpu
from jax.sharding import PartitionSpec as P


ORDER = 10
LEVELS = 17
MIDDLE = (LEVELS - 1) // 2
BF16 = jnp.bfloat16
F32 = jnp.float32
VMEM = pl.BlockSpec(memory_space=pltpu.VMEM)


def call(kernel, out_shape, count, scratch=(), passes=0, scalars=0):
    return pl.pallas_call(
        kernel,
        out_shape=out_shape,
        in_specs=[pl.BlockSpec(memory_space=pltpu.SMEM)] * scalars + [VMEM] * count,
        out_specs=jax.tree.map(lambda _: VMEM, out_shape),
        scratch_shapes=list(scratch),
        compiler_params=pltpu.CompilerParams(vmem_limit_bytes=16 << 20),
        cost_estimate=pl.CostEstimate(flops=passes, transcendentals=0, bytes_accessed=0) if passes else None,
    )


def shape(rows, columns, kind=F32):
    return jax.ShapeDtypeStruct((rows, columns), kind)


def split(value):
    high = value.astype(BF16)
    return high, (value - high.astype(F32)).astype(BF16)


def dot3(left, right):
    def dot(a, b):
        return jnp.dot(a, b, preferred_element_type=F32)

    return dot(left[0], right[0]) + (dot(left[1], right[0]) + dot(left[0], right[1]))


def prepare_kernel(hop_x_ref, hop_y_ref, xh_ref, xl_ref, yh_ref, yl_ref):
    for ref, high_ref, low_ref in ((hop_x_ref, xh_ref, xl_ref), (hop_y_ref, yh_ref, yl_ref)):
        side = ref.shape[0]
        hop = ref[...]
        square = jnp.dot(hop, hop, precision=lax.Precision.HIGHEST, preferred_element_type=F32)
        high_ref[:side], low_ref[:side] = split(hop)
        high_ref[side:], low_ref[side:] = split(square)


def transform_kernel(block_ref, th_ref, tl_ref, out_ref):
    rows, columns = block_ref.shape
    block = split(block_ref[...])
    result = dot3((th_ref[...], tl_ref[...]), block)
    for part in range(th_ref.shape[0] // rows):
        out_ref[:, part * columns : (part + 1) * columns] = result[part * rows : (part + 1) * rows]


def chebyshev_kernel(*refs):
    field_ref, xh_ref, xl_ref, yh_ref, yl_ref, sum_ref, cos_ref = refs[:7]
    add_ref = refs[7] if len(refs) == 10 else None
    out_ref, weight_ref = refs[-2:]
    side_x = field_ref.shape[0]
    side_y = field_ref.shape[1]
    mean_level = jnp.sum(sum_ref[...], axis=0, keepdims=True)
    cbar = jnp.exp(-0.05 * (mean_level - MIDDLE))
    lower = 0.05
    root_lower = math.sqrt(lower)
    root_upper = 1.0 + 3.0 * cbar
    upper = root_upper * root_upper
    spread = upper - lower
    ratio = (root_upper - root_lower) / (root_upper + root_lower)
    keep = 2.0 * (2.0 - (upper + lower)) / spread
    once = -8.0 * cos_ref[...] * cbar / spread
    twice = 4.0 * cbar * cbar / spread
    weight = 2.0 / (root_upper * root_lower)
    for degree in range(ORDER + 1):
        weight_ref[degree : degree + 1, :] = weight
        weight = weight * -ratio
    field = field_ref[...]
    half = side_x // 2

    def left(start, value):
        window = slice(start, start + half)
        return dot3((xh_ref[window], xl_ref[window]), value)

    def body(index, carry):
        ahead, second, _ = carry
        value = split(ahead)
        row = weight_ref[pl.ds(ORDER - 1 - index, 1), :]
        inner = [
            (split(left(start, value) * once), split(left(side_x + start, value) * twice)) for start in (0, half)
        ]
        parts = []
        for start, (single, double) in zip((0, half), inner):
            window = slice(start, start + half)
            hops = dot3(single, (yh_ref[:side_y], yl_ref[:side_y])) + dot3(double, (yh_ref[side_y:], yl_ref[side_y:]))
            parts.append((row * field[window] + keep * ahead[window] - second[window]) + hops)
        return jnp.concatenate(parts, axis=0), ahead, second

    ahead = weight_ref[ORDER : ORDER + 1, :] * field
    before = ahead - ahead
    result, _, second = lax.fori_loop(0, ORDER, body, (ahead, before, before), unroll=ORDER // 2)
    total = 0.5 * (result - second)
    out_ref[...] = total if add_ref is None else total + add_ref[...]


def residual_parts(before, here, after, damp, damp_next, noise_ref, x_refs, y_refs, out_ref):
    side_x, side_y = here.shape
    half = side_x // 2
    windows = (slice(0, half), slice(half, side_x))
    y_pair = tuple(ref[:side_y] for ref in y_refs)

    def propagate(value):
        value = split(value)
        inner = [split(dot3((x_refs[0][window], x_refs[1][window]), value)) for window in windows]
        return [dot3(part, y_pair) for part in inner]

    moved = propagate(damp_next * here)
    forward_next = jnp.concatenate([after[window] - part for window, part in zip(windows, moved)], axis=0)
    moved = propagate(damp * before)
    carried = propagate(forward_next)
    for window, part, back in zip(windows, moved, carried):
        forward = here[window] - part
        out_ref[window] = noise_ref[window] - (forward - damp_next[window] * back)


def normal_kernel(
    even_ref, slices_ref, other_ref, damp_ref, damp_next_ref, noise_ref, xh_ref, xl_ref, yh_ref, yl_ref, out_ref
):
    side_y = other_ref.shape[1]
    even = even_ref[...] > 0.5
    far = slices_ref[:, :side_y]
    here = slices_ref[:, side_y:]
    near = other_ref[...]
    before = jnp.where(even, far, near)
    after = jnp.where(even, near, far)
    damps = damp_ref[...], damp_next_ref[...]
    residual_parts(before, here, after, *damps, noise_ref, (xh_ref, xl_ref), (yh_ref, yl_ref), out_ref)


def gather_kernel(*refs):
    weight_ref, keep_ref, send_ref = refs[0], refs[-2], refs[-1]
    field_refs = refs[1:-2]
    side_x, side_y = field_refs[0].shape
    count = len(field_refs)
    rows = 16

    def body(index, carry):
        window = pl.ds(pl.multiple_of(index * rows, rows), rows)
        fields = [ref[window, :] for ref in field_refs]
        for part in range(6):
            total = weight_ref[part * count] * fields[0]
            for place in range(1, count):
                total = total + weight_ref[part * count + place] * fields[place]
            target = keep_ref if part < 3 else send_ref
            target[window, (part % 3) * side_y : (part % 3 + 1) * side_y] = total
        return carry

    lax.fori_loop(0, side_x // rows, body, 0, unroll=4)


def finish_kernel(*refs):
    weight_ref, keep_ref, other_ref = refs[:3]
    low_ref, high_ref, low_other_ref, high_other_ref = refs[3:7]
    damp_ref, damp_next_ref, noise_ref, xh_ref, xl_ref, yh_ref, yl_ref = refs[7:14]
    out_refs = refs[14:]
    side_y = damp_ref.shape[1]
    last = jnp.concatenate([low_ref[...], high_ref[...]], axis=0)
    last_other = jnp.concatenate([low_other_ref[...], high_other_ref[...]], axis=0)
    slices = []
    for part in range(3):
        window = slice(part * side_y, (part + 1) * side_y)
        total = keep_ref[:, window] + other_ref[:, window]
        slices.append(total + (weight_ref[2 * part] * last + weight_ref[2 * part + 1] * last_other))
    if len(out_refs) == 2:
        out_refs[1][...] = slices[1]
    damps = damp_ref[...], damp_next_ref[...]
    residual_parts(*slices, *damps, noise_ref, (xh_ref, xl_ref), (yh_ref, yl_ref), out_refs[0])


def basis_of(length):
    times = np.arange(length)
    phase = (2 * (times // 2)[:, None] + 1) * times[None, :] % (2 * length)
    angles = phase * (math.pi / length)
    basis = np.where((times % 2 == 0)[:, None], np.cos(angles), np.sin(angles))
    return basis, basis.T * (2.0 / length)


def times_of(inverse, slices):
    length = inverse.shape[0]
    outside = (slices < 0) | (slices >= length)
    return inverse[slices % length] * np.where(outside, -1.0, 1.0)[:, None]


def table_parts(matrix, rows):
    matrix = np.kron(matrix, np.eye(rows))
    high = matrix.astype(BF16)
    return jnp.asarray(high), jnp.asarray((matrix - high.astype(np.float64)).astype(BF16))


def ring_of(length):
    chips = length // 2
    return [*range(0, chips, 2), *reversed(range(1, chips, 2))]


def ring_pairs(length, direction):
    path = ring_of(length)
    chips = len(path)
    return [
        (2 * path[i] + core, 2 * path[(i + direction) % chips] + core) for i in range(chips) for core in range(2)
    ]


def ring_weights(length):
    _, inverse = basis_of(length)
    path = ring_of(length)
    chips = len(path)
    reach = chips // 2
    offsets = [0] + [sign * hop for hop in range(1, reach) for sign in (-1, 1)]
    gathers, finishes = [], []
    for device in range(length):
        core = device % 2
        place = path.index(device // 2)
        arrivals = [2 * path[(place + offset) % chips] + core for offset in offsets]
        own = times_of(inverse, np.arange(device - 1, device + 2))
        partner = times_of(inverse, np.arange((device ^ 1) - 1, (device ^ 1) + 2))
        far = 2 * path[(place + reach) % chips]
        gathers.append(np.concatenate([own[:, arrivals].ravel(), partner[:, arrivals].ravel()]))
        finishes.append(own[:, [far + core, far + 1 - core]].ravel())
    return np.stack(gathers).astype(np.float32), np.stack(finishes).astype(np.float32)


def add_partners(value, axis, step):
    count = lax.axis_size(axis)
    value = jnp.sum(value, axis=0, keepdims=True)
    shifts = range(1, min(4, count // step))
    others = [lax.ppermute(value, axis, [(i, i ^ (step * shift)) for i in range(count)]) for shift in shifts]
    return jnp.concatenate([value] + others, axis=0)


def exchange(value, axis):
    count = lax.axis_size(axis)
    rows, columns = value.shape
    blocks = value.reshape(count, rows // count, columns)
    return lax.all_to_all(blocks, axis, split_axis=0, concat_axis=0, tiled=True).reshape(rows, columns)


def per_device(noise, phonon_level, hop_x, hop_y):
    _, side_x, side_y = noise.shape
    length = lax.axis_size("tm")
    position = lax.axis_index("tm")
    noise = noise[0]
    levels = phonon_level[0].astype(F32)
    damp = jnp.exp(-0.05 * (levels - MIDDLE))
    mean_rows = jnp.full((1, side_y), jnp.sum(levels) / (length * side_x * side_y), F32)
    cosine = jnp.cos((2 * (position // 2) + 1).astype(F32) * (math.pi / length))
    cosine = jnp.full((1, side_y), cosine, F32)
    basis, inverse = basis_of(length)
    forward = table_parts(basis, side_x // length)
    chips = length // 2
    ring = length % 4 == 0 and 4 <= chips <= 8 and side_x % 16 == 0

    hops = call(prepare_kernel, (shape(2 * side_x, side_x, BF16),) * 2 + (shape(2 * side_y, side_y, BF16),) * 2, 2)(
        hop_x, hop_y
    )
    field_shape = shape(side_x, side_y)
    to_spectrum = call(transform_kernel, field_shape, 3)
    work = 12 * ORDER * 2 * side_x * side_y * max(side_x, side_y)

    def chebyshev(*operands):
        return call(chebyshev_kernel, field_shape, len(operands), [pltpu.VMEM((16, side_y), F32)], work)(*operands)

    def spectrum(field, beside):
        block = to_spectrum(exchange(field, "tm"), *forward)
        block, beside = lax.optimization_barrier((block, beside))
        return exchange(block, "tm"), beside

    def by_exchange(components, turn):
        times = np.arange(length)
        far = times_of(inverse, np.where(times % 2 == 0, times - 1, times + 1))
        back = [
            jnp.concatenate(pair, axis=0)
            for pair in zip(table_parts(far, side_x // length), table_parts(inverse, side_x // length))
        ]
        block = exchange(components, "tm")
        slices = exchange(call(transform_kernel, shape(side_x, 2 * side_y), 3)(block, *back), "tm")
        here = slices[:, side_y:]
        other = lax.ppermute(here, "tm", swap)
        even = jnp.full((1, side_y), (position % 2 == 0).astype(F32), F32)
        residual = call(normal_kernel, field_shape, 10)(even, slices, other, damp, damp_next, noise, *hops)
        return (residual, here) if turn else (residual,)

    def by_ring(components, turn):
        gather_weights, finish_weights = (
            lax.dynamic_index_in_dim(jnp.asarray(table), position, 0, keepdims=False) for table in ring_weights(length)
        )
        up, down = ring_pairs(length, 1), ring_pairs(length, -1)
        going_up = going_down = components
        arrived = [components]
        for _ in range(chips // 2 - 1):
            going_up = lax.ppermute(going_up, "tm", up)
            going_down = lax.ppermute(going_down, "tm", down)
            arrived += [going_up, going_down]
        half = side_x // 2
        low = lax.ppermute(going_up[:half], "tm", up)
        high = lax.ppermute(going_down[half:], "tm", down)
        wide = shape(side_x, 3 * side_y)
        adds = 2 * 6 * len(arrived) * side_x * side_y
        gather = call(gather_kernel, (wide, wide), len(arrived), passes=adds, scalars=1)
        keep, send = gather(gather_weights, *arrived)
        other = lax.ppermute(send, "tm", swap)
        low_other = lax.ppermute(low, "tm", swap)
        high_other = lax.ppermute(high, "tm", swap)
        outs = (field_shape,) * (2 if turn else 1)
        return call(finish_kernel, outs, 13, scalars=1)(
            finish_weights, keep, other, low, high, low_other, high_other, damp, damp_next, noise, *hops
        )

    swap = [(i, i ^ 1) for i in range(length)]
    residual_of = by_ring if ring else by_exchange

    power_of_two = length & (length - 1) == 0
    mean_rows = add_partners(mean_rows, "tm", 1) if power_of_two else lax.psum(mean_rows, "tm")
    field, mean_rows = spectrum(noise, mean_rows)
    step = 4
    while power_of_two and step < length:
        mean_rows = add_partners(mean_rows, "tm", step)
        step *= 4
    field, damp = lax.optimization_barrier((field, damp))
    damp_next = lax.ppermute(damp, "tm", [(i, (i - 1) % length) for i in range(length)])
    first = chebyshev(field, *hops, mean_rows, cosine)
    first, damp_next = lax.optimization_barrier((first, damp_next))

    (second_residual,) = residual_of(first, 0)
    field, _ = spectrum(second_residual, cosine)
    total = chebyshev(field, *hops, mean_rows, cosine, first)
    residual, result = residual_of(total, 1)
    return result[None], residual[None]


def solution(mesh):
    return jax.shard_map(
        per_device,
        mesh=mesh,
        in_specs=(P(("grp", "tm"), None, None), P(("grp", "tm"), None, None), P(), P()),
        out_specs=(P(("grp", "tm"), None, None), P(("grp", "tm"), None, None)),
        check_vma=False,
    )
```

```python
import math

import jax
import jax.numpy as jnp
import numpy as np
from jax import lax
from jax.experimental import pallas as pl
from jax.experimental.pallas import tpu as pltpu
from jax.sharding import PartitionSpec as P


ORDER = 10
LEVELS = 17
MIDDLE = (LEVELS - 1) // 2
BF16 = jnp.bfloat16
F32 = jnp.float32
VMEM = pl.BlockSpec(memory_space=pltpu.VMEM)


def call(kernel, out_shape, count, scratch=(), passes=0, scalars=0):
    return pl.pallas_call(
        kernel,
        out_shape=out_shape,
        in_specs=[pl.BlockSpec(memory_space=pltpu.SMEM)] * scalars + [VMEM] * count,
        out_specs=jax.tree.map(lambda _: VMEM, out_shape),
        scratch_shapes=list(scratch),
        compiler_params=pltpu.CompilerParams(vmem_limit_bytes=16 << 20),
        cost_estimate=pl.CostEstimate(flops=passes, transcendentals=0, bytes_accessed=0) if passes else None,
    )


def shape(rows, columns, kind=F32):
    return jax.ShapeDtypeStruct((rows, columns), kind)


def split(value):
    high = value.astype(BF16)
    return high, (value - high.astype(F32)).astype(BF16)


def dot3(left, right):
    def dot(a, b):
        return jnp.dot(a, b, preferred_element_type=F32)

    return dot(left[0], right[0]) + (dot(left[1], right[0]) + dot(left[0], right[1]))


def prepare_kernel(hop_x_ref, hop_y_ref, xh_ref, xl_ref, yh_ref, yl_ref):
    for ref, high_ref, low_ref in ((hop_x_ref, xh_ref, xl_ref), (hop_y_ref, yh_ref, yl_ref)):
        side = ref.shape[0]
        hop = ref[...]
        square = jnp.dot(hop, hop, precision=lax.Precision.HIGHEST, preferred_element_type=F32)
        high_ref[:side], low_ref[:side] = split(hop)
        high_ref[side:], low_ref[side:] = split(square)


def transform_kernel(block_ref, th_ref, tl_ref, out_ref):
    rows, columns = block_ref.shape
    block = split(block_ref[...])
    result = dot3((th_ref[...], tl_ref[...]), block)
    for part in range(th_ref.shape[0] // rows):
        out_ref[:, part * columns : (part + 1) * columns] = result[part * rows : (part + 1) * rows]


def chebyshev_sum(field, mean_level, cos_ref, hop_refs, weight_ref):
    xh_ref, xl_ref, yh_ref, yl_ref = hop_refs
    side_x, side_y = field.shape
    cbar = jnp.exp(-0.05 * (mean_level - MIDDLE))
    lower = 0.05
    root_lower = math.sqrt(lower)
    root_upper = 1.0 + 3.0 * cbar
    upper = root_upper * root_upper
    spread = upper - lower
    ratio = (root_upper - root_lower) / (root_upper + root_lower)
    keep = 2.0 * (2.0 - (upper + lower)) / spread
    once = -8.0 * cos_ref[...] * cbar / spread
    twice = 4.0 * cbar * cbar / spread
    weight = 2.0 / (root_upper * root_lower)
    for degree in range(ORDER + 1):
        weight_ref[degree : degree + 1, :] = weight
        weight = weight * -ratio
    half = side_x // 2

    def left(start, value):
        window = slice(start, start + half)
        return dot3((xh_ref[window], xl_ref[window]), value)

    def body(index, carry):
        ahead, second, _ = carry
        value = split(ahead)
        row = weight_ref[pl.ds(ORDER - 1 - index, 1), :]
        inner = [
            (split(left(start, value) * once), split(left(side_x + start, value) * twice)) for start in (0, half)
        ]
        parts = []
        for start, (single, double) in zip((0, half), inner):
            window = slice(start, start + half)
            hops = dot3(single, (yh_ref[:side_y], yl_ref[:side_y])) + dot3(double, (yh_ref[side_y:], yl_ref[side_y:]))
            parts.append((row * field[window] + keep * ahead[window] - second[window]) + hops)
        return jnp.concatenate(parts, axis=0), ahead, second

    ahead = weight_ref[ORDER : ORDER + 1, :] * field
    before = ahead - ahead
    result, _, second = lax.fori_loop(0, ORDER, body, (ahead, before, before), unroll=ORDER // 2)
    return 0.5 * (result - second)


def chebyshev_kernel(*refs):
    field_ref, sum_ref, cos_ref = refs[:3]
    out_ref, weight_ref = refs[-2:]
    mean_level = jnp.sum(sum_ref[...], axis=0, keepdims=True)
    total = chebyshev_sum(field_ref[...], mean_level, cos_ref, refs[3:7], weight_ref)
    out_ref[...] = total if len(refs) == 9 else total + refs[7][...]


def joined(weight_ref, part, refs, window):
    keep_ref, other_ref, last_ref, last_other_ref = refs
    side_y = last_ref.shape[1]
    columns = slice(part * side_y, (part + 1) * side_y)
    total = keep_ref[window, columns] + other_ref[window, columns]
    return total + (weight_ref[2 * part] * last_ref[window] + weight_ref[2 * part + 1] * last_other_ref[window])


def first_spectral_kernel(weight_ref, keep_ref, other_ref, last_ref, last_other_ref, cos_ref, *refs):
    hop_refs, (out_ref, mean_ref, row_ref) = refs[:4], refs[4:]
    side_x = out_ref.shape[0]
    sources = keep_ref, other_ref, last_ref, last_other_ref
    row = sum(ref[side_x : side_x + 1, :] for ref in sources)
    mean_level = jnp.broadcast_to(jnp.sum(row, axis=1, keepdims=True), row.shape)
    mean_ref[...] = mean_level
    field = joined(weight_ref, 0, sources, slice(0, side_x))
    out_ref[...] = chebyshev_sum(field, mean_level, cos_ref, hop_refs, row_ref)


def next_spectral_kernel(weight_ref, keep_ref, other_ref, last_ref, last_other_ref, cos_ref, *refs):
    hop_refs, (mean_ref, add_ref, out_ref, row_ref) = refs[:4], refs[4:]
    field = joined(weight_ref, 0, (keep_ref, other_ref, last_ref, last_other_ref), slice(None))
    out_ref[...] = chebyshev_sum(field, mean_ref[...], cos_ref, hop_refs, row_ref) + add_ref[...]


def pack_kernel(noise_ref, level_ref, packed_ref, damp_ref, *, scale):
    side_x = noise_ref.shape[0]
    levels = level_ref[...].astype(F32)
    damp_ref[...] = jnp.exp(-0.05 * (levels - MIDDLE))
    packed_ref[:side_x] = noise_ref[...]
    share = jnp.sum(levels, axis=0, keepdims=True) * scale
    packed_ref[side_x:] = jnp.broadcast_to(share, (packed_ref.shape[0] - side_x, share.shape[1]))


def residual_parts(before, here, after, damp, damp_next, noise_ref, x_refs, y_refs, out_ref):
    side_x, side_y = here.shape
    half = side_x // 2
    windows = (slice(0, half), slice(half, side_x))
    y_pair = tuple(ref[:side_y] for ref in y_refs)

    def propagate(value):
        value = split(value)
        inner = [split(dot3((x_refs[0][window], x_refs[1][window]), value)) for window in windows]
        return [dot3(part, y_pair) for part in inner]

    moved = propagate(damp_next * here)
    forward_next = jnp.concatenate([after[window] - part for window, part in zip(windows, moved)], axis=0)
    moved = propagate(damp * before)
    carried = propagate(forward_next)
    for window, part, back in zip(windows, moved, carried):
        forward = here[window] - part
        out_ref[window] = noise_ref[window] - (forward - damp_next[window] * back)


def normal_kernel(
    even_ref, slices_ref, other_ref, damp_ref, damp_next_ref, noise_ref, xh_ref, xl_ref, yh_ref, yl_ref, out_ref
):
    side_y = other_ref.shape[1]
    even = even_ref[...] > 0.5
    far = slices_ref[:, :side_y]
    here = slices_ref[:, side_y:]
    near = other_ref[...]
    before = jnp.where(even, far, near)
    after = jnp.where(even, near, far)
    damps = damp_ref[...], damp_next_ref[...]
    residual_parts(before, here, after, *damps, noise_ref, (xh_ref, xl_ref), (yh_ref, yl_ref), out_ref)


def gather_kernel(*refs, outs, side_x):
    weight_ref, keep_ref, send_ref = refs[0], refs[-2], refs[-1]
    field_refs = refs[1:-2]
    rows_in, side_y = field_refs[0].shape
    count = len(field_refs)
    rows = 16

    def body(index, carry):
        window = pl.ds(pl.multiple_of(index * rows, rows), rows)
        fields = [ref[window, :] for ref in field_refs]
        for target, start, base in ((keep_ref, 0, 0), (send_ref, 2, outs * count)):
            for part in range(outs):
                place = base + part * (count - start) - start
                total = weight_ref[place + start] * fields[start]
                for index_in in range(start + 1, count):
                    total = total + weight_ref[place + index_in] * fields[index_in]
                target[window, part * side_y : (part + 1) * side_y] = total
        return carry

    lax.fori_loop(0, side_x // rows, body, 0, unroll=4)
    if rows_in > side_x:
        extra = [ref[side_x:, :] for ref in field_refs]
        keep_ref[side_x:, :] = sum(extra)
        send_ref[side_x:, :] = sum(extra[2:])


def finish_kernel(weight_ref, keep_ref, other_ref, last_ref, last_other_ref, *refs):
    damp_ref, damp_next_ref, noise_ref, xh_ref, xl_ref, yh_ref, yl_ref = refs[:7]
    out_refs = refs[7:]
    sources = keep_ref, other_ref, last_ref, last_other_ref
    slices = [joined(weight_ref, part, sources, slice(None)) for part in range(3)]
    if len(out_refs) == 2:
        out_refs[1][...] = slices[1]
    damps = damp_ref[...], damp_next_ref[...]
    residual_parts(*slices, *damps, noise_ref, (xh_ref, xl_ref), (yh_ref, yl_ref), out_refs[0])


def basis_of(length):
    times = np.arange(length)
    phase = (2 * (times // 2)[:, None] + 1) * times[None, :] % (2 * length)
    angles = phase * (math.pi / length)
    basis = np.where((times % 2 == 0)[:, None], np.cos(angles), np.sin(angles))
    return basis, basis.T * (2.0 / length)


def times_of(inverse, slices):
    length = inverse.shape[0]
    outside = (slices < 0) | (slices >= length)
    return inverse[slices % length] * np.where(outside, -1.0, 1.0)[:, None]


def table_parts(matrix, rows):
    matrix = np.kron(matrix, np.eye(rows))
    high = matrix.astype(BF16)
    return jnp.asarray(high), jnp.asarray((matrix - high.astype(np.float64)).astype(BF16))


def ring_of(length):
    chips = length // 2
    return [*range(0, chips, 2), *reversed(range(1, chips, 2))]


def ring_pairs(length):
    path = ring_of(length)
    chips = len(path)
    pairs = []
    for place, chip in enumerate(path):
        pairs += [(2 * chip, 2 * path[(place + 1) % chips]), (2 * chip + 1, 2 * path[place - 1] + 1)]
    return pairs


def ring_weights(length, rows_of):
    path = ring_of(length)
    chips = len(path)
    reach = chips // 2
    gathers, finishes = [], []
    for device in range(length):
        core = device % 2
        place = path.index(device // 2)
        way = 1 - 2 * core
        own, partner = rows_of(device), rows_of(device ^ 1)
        arrivals = [
            2 * path[(place - way * hop) % chips] + side for hop in range(reach) for side in (core, 1 - core)
        ]
        far = 2 * path[(place + reach) % chips]
        gathers.append(np.concatenate([own[:, arrivals].ravel(), partner[:, arrivals[2:]].ravel()]))
        finishes.append(own[:, [far + core, far + 1 - core]].ravel())
    return np.stack(gathers).astype(np.float32), np.stack(finishes).astype(np.float32)


def add_partners(value, axis, step):
    count = lax.axis_size(axis)
    value = jnp.sum(value, axis=0, keepdims=True)
    shifts = range(1, min(4, count // step))
    others = [lax.ppermute(value, axis, [(i, i ^ (step * shift)) for i in range(count)]) for shift in shifts]
    return jnp.concatenate([value] + others, axis=0)


def exchange(value, axis):
    count = lax.axis_size(axis)
    rows, columns = value.shape
    blocks = value.reshape(count, rows // count, columns)
    return lax.all_to_all(blocks, axis, split_axis=0, concat_axis=0, tiled=True).reshape(rows, columns)


def by_exchange(noise, phonon_level, hops, cosine):
    side_x, side_y = noise.shape
    length = lax.axis_size("tm")
    position = lax.axis_index("tm")
    rows = side_x // length
    field_shape = shape(side_x, side_y)
    levels = phonon_level.astype(F32)
    damp = jnp.exp(-0.05 * (levels - MIDDLE))
    mean_rows = jnp.full((1, side_y), jnp.sum(levels) / (length * side_x * side_y), F32)
    basis, inverse = basis_of(length)
    forward = table_parts(basis, rows)
    times = np.arange(length)
    far = times_of(inverse, np.where(times % 2 == 0, times - 1, times + 1))
    back = [jnp.concatenate(pair, axis=0) for pair in zip(table_parts(far, rows), table_parts(inverse, rows))]

    def chebyshev(field, *operands):
        scratch = [pltpu.VMEM((16, side_y), F32)]
        return call(chebyshev_kernel, field_shape, 7 + len(operands), scratch)(field, mean_rows, cosine, *hops, *operands)

    def spectrum(field, beside):
        block = call(transform_kernel, field_shape, 3)(exchange(field, "tm"), *forward)
        block, beside = lax.optimization_barrier((block, beside))
        return exchange(block, "tm"), beside

    def residual_of(components):
        block = exchange(components, "tm")
        slices = exchange(call(transform_kernel, shape(side_x, 2 * side_y), 3)(block, *back), "tm")
        here = slices[:, side_y:]
        other = lax.ppermute(here, "tm", [(i, i ^ 1) for i in range(length)])
        even = jnp.full((1, side_y), (position % 2 == 0).astype(F32), F32)
        return here, call(normal_kernel, field_shape, 10)(even, slices, other, damp, damp_next, noise, *hops)

    power_of_two = length & (length - 1) == 0
    mean_rows = add_partners(mean_rows, "tm", 1) if power_of_two else lax.psum(mean_rows, "tm")
    field, mean_rows = spectrum(noise, mean_rows)
    step = 4
    while power_of_two and step < length:
        mean_rows = add_partners(mean_rows, "tm", step)
        step *= 4
    damp_next = lax.ppermute(damp, "tm", [(i, (i - 1) % length) for i in range(length)])
    first = chebyshev(field)
    _, second_residual = residual_of(first)
    field, _ = spectrum(second_residual, cosine)
    return residual_of(chebyshev(field, first))


def by_ring(noise, phonon_level, hops, cosine):
    side_x, side_y = noise.shape
    length = lax.axis_size("tm")
    position = lax.axis_index("tm")
    reach = length // 4
    extra = 8
    field_shape = shape(side_x, side_y)
    basis, inverse = basis_of(length)
    hop = ring_pairs(length)
    swap = [(i, i ^ 1) for i in range(length)]

    def weights_of(rows_of):
        tables = ring_weights(length, rows_of)
        return [lax.dynamic_index_in_dim(jnp.asarray(table), position, 0, keepdims=False) for table in tables]

    forward = weights_of(lambda device: basis[device : device + 1])
    back = weights_of(lambda device: times_of(inverse, np.arange(device - 1, device + 2)))

    def around(own, weights, outs):
        partner = lax.ppermute(own, "tm", swap)
        fields = [own, partner]
        for _ in range(reach - 1):
            own = lax.ppermute(own, "tm", hop)
            partner = lax.ppermute(partner, "tm", hop)
            fields += [own, partner]
        last = lax.ppermute(own, "tm", hop)

        def kernel(*refs):
            gather_kernel(*refs, outs=outs, side_x=side_x)

        wide = shape(own.shape[0], outs * side_y)
        adds = 4 * outs * len(fields) * side_x * side_y
        keep, send = call(kernel, (wide, wide), len(fields), passes=adds, scalars=1)(weights[0], *fields)
        other = lax.ppermute(send, "tm", swap)
        last_other = lax.ppermute(last, "tm", swap)
        return weights[1], keep, other, last, last_other

    scratch = [pltpu.VMEM((16, side_y), F32)]
    work = 12 * ORDER * 2 * side_x * side_y * max(side_x, side_y)

    def pack(*refs):
        pack_kernel(*refs, scale=1.0 / (length * side_x * side_y))

    packed, damp = call(pack, (shape(side_x + extra, side_y), field_shape), 2)(noise, phonon_level)
    parts = around(packed, forward, 1)
    parts, damp_late = lax.optimization_barrier((parts, damp))
    damp_next = lax.ppermute(damp_late, "tm", [(i, (i - 1) % length) for i in range(length)])
    first_outs = (field_shape, shape(1, side_y))
    first, mean_level = call(first_spectral_kernel, first_outs, 9, scratch, work, 1)(*parts, cosine, *hops)
    first, damp_next = lax.optimization_barrier((first, damp_next))
    parts = around(first, back, 3)
    (second_residual,) = call(finish_kernel, (field_shape,), 11, scalars=1)(*parts, damp, damp_next, noise, *hops)
    parts = around(second_residual, forward, 1)
    total = call(next_spectral_kernel, field_shape, 11, scratch, work, 1)(*parts, cosine, *hops, mean_level, first)
    parts = around(total, back, 3)
    residual, result = call(finish_kernel, (field_shape,) * 2, 11, scalars=1)(*parts, damp, damp_next, noise, *hops)
    return result, residual


def per_device(noise, phonon_level, hop_x, hop_y):
    _, side_x, side_y = noise.shape
    length = lax.axis_size("tm")
    position = lax.axis_index("tm")
    cosine = jnp.cos((2 * (position // 2) + 1).astype(F32) * (math.pi / length))
    cosine = jnp.full((1, side_y), cosine, F32)
    hop_parts = (shape(2 * side_x, side_x, BF16),) * 2 + (shape(2 * side_y, side_y, BF16),) * 2
    hops = call(prepare_kernel, hop_parts, 2)(hop_x, hop_y)
    ring = length % 4 == 0 and 8 <= length <= 16 and side_x % 64 == 0
    result, residual = (by_ring if ring else by_exchange)(noise[0], phonon_level[0], hops, cosine)
    return result[None], residual[None]


def solution(mesh):
    return jax.shard_map(
        per_device,
        mesh=mesh,
        in_specs=(P(("grp", "tm"), None, None), P(("grp", "tm"), None, None), P(), P()),
        out_specs=(P(("grp", "tm"), None, None), P(("grp", "tm"), None, None)),
        check_vma=False,
    )
```

```python
import math

import jax
import jax.numpy as jnp
import numpy as np
from jax import lax
from jax.experimental import pallas as pl
from jax.experimental.pallas import tpu as pltpu
from jax.sharding import PartitionSpec as P


ORDER = 10
LEVELS = 17
MIDDLE = (LEVELS - 1) // 2
BF16 = jnp.bfloat16
F32 = jnp.float32
VMEM = pl.BlockSpec(memory_space=pltpu.VMEM)


def call(kernel, out_shape, count, scratch=(), passes=0, scalars=0):
    return pl.pallas_call(
        kernel,
        out_shape=out_shape,
        in_specs=[pl.BlockSpec(memory_space=pltpu.SMEM)] * scalars + [VMEM] * count,
        out_specs=jax.tree.map(lambda _: VMEM, out_shape),
        scratch_shapes=list(scratch),
        compiler_params=pltpu.CompilerParams(vmem_limit_bytes=16 << 20),
        cost_estimate=pl.CostEstimate(flops=passes, transcendentals=0, bytes_accessed=0) if passes else None,
    )


def shape(rows, columns, kind=F32):
    return jax.ShapeDtypeStruct((rows, columns), kind)


def split(value):
    high = value.astype(BF16)
    return high, (value - high.astype(F32)).astype(BF16)


def dot3(left, right):
    def dot(a, b):
        return jnp.dot(a, b, preferred_element_type=F32)

    return dot(left[0], right[0]) + (dot(left[1], right[0]) + dot(left[0], right[1]))


def prepare_kernel(hop_x_ref, hop_y_ref, xh_ref, xl_ref, yh_ref, yl_ref):
    for ref, high_ref, low_ref in ((hop_x_ref, xh_ref, xl_ref), (hop_y_ref, yh_ref, yl_ref)):
        side = ref.shape[0]
        hop = ref[...]
        square = jnp.dot(hop, hop, precision=lax.Precision.HIGHEST, preferred_element_type=F32)
        high_ref[:side], low_ref[:side] = split(hop)
        high_ref[side:], low_ref[side:] = split(square)


def transform_kernel(block_ref, th_ref, tl_ref, out_ref):
    rows, columns = block_ref.shape
    block = split(block_ref[...])
    result = dot3((th_ref[...], tl_ref[...]), block)
    for part in range(th_ref.shape[0] // rows):
        out_ref[:, part * columns : (part + 1) * columns] = result[part * rows : (part + 1) * rows]


def chebyshev_sum(field, mean_level, cos_ref, hop_refs, weight_ref):
    xh_ref, xl_ref, yh_ref, yl_ref = hop_refs
    side_x, side_y = field.shape
    cbar = jnp.exp(-0.05 * (mean_level - MIDDLE))
    lower = 0.05
    root_lower = math.sqrt(lower)
    root_upper = 1.0 + 3.0 * cbar
    upper = root_upper * root_upper
    spread = upper - lower
    ratio = (root_upper - root_lower) / (root_upper + root_lower)
    keep = 2.0 * (2.0 - (upper + lower)) / spread
    once = -8.0 * cos_ref[...] * cbar / spread
    twice = 4.0 * cbar * cbar / spread
    weight = 2.0 / (root_upper * root_lower)
    for degree in range(ORDER + 1):
        weight_ref[degree : degree + 1, :] = weight
        weight = weight * -ratio
    half = side_x // 2

    def left(start, value):
        window = slice(start, start + half)
        return dot3((xh_ref[window], xl_ref[window]), value)

    def body(index, carry):
        ahead, second, _ = carry
        value = split(ahead)
        row = weight_ref[pl.ds(ORDER - 1 - index, 1), :]
        inner = [
            (split(left(start, value) * once), split(left(side_x + start, value) * twice)) for start in (0, half)
        ]
        parts = []
        for start, (single, double) in zip((0, half), inner):
            window = slice(start, start + half)
            hops = dot3(single, (yh_ref[:side_y], yl_ref[:side_y])) + dot3(double, (yh_ref[side_y:], yl_ref[side_y:]))
            parts.append((row * field[window] + keep * ahead[window] - second[window]) + hops)
        return jnp.concatenate(parts, axis=0), ahead, second

    ahead = weight_ref[ORDER : ORDER + 1, :] * field
    before = ahead - ahead
    result, _, second = lax.fori_loop(0, ORDER, body, (ahead, before, before), unroll=ORDER // 2)
    return 0.5 * (result - second)


def chebyshev_kernel(*refs):
    field_ref, sum_ref, cos_ref = refs[:3]
    out_ref, weight_ref = refs[-2:]
    mean_level = jnp.sum(sum_ref[...], axis=0, keepdims=True)
    total = chebyshev_sum(field_ref[...], mean_level, cos_ref, refs[3:7], weight_ref)
    out_ref[...] = total if len(refs) == 9 else total + refs[7][...]


def joined(weight_ref, base, part, refs, window):
    keep_ref, other_ref, last_ref, last_other_ref = refs
    side_y = last_ref.shape[1]
    columns = slice(part * side_y, (part + 1) * side_y)
    total = keep_ref[window, columns] + other_ref[window, columns]
    return total + (weight_ref[base + 2 * part] * last_ref[window] + weight_ref[base + 2 * part + 1] * last_other_ref[window])


def first_spectral_kernel(weight_ref, base, keep_ref, other_ref, last_ref, last_other_ref, cos_ref, *refs):
    hop_refs, (out_ref, mean_ref, row_ref) = refs[:4], refs[4:]
    side_x = out_ref.shape[0]
    sources = keep_ref, other_ref, last_ref, last_other_ref
    row = sum(ref[side_x : side_x + 1, :] for ref in sources)
    mean_level = jnp.broadcast_to(jnp.sum(row, axis=1, keepdims=True), row.shape)
    mean_ref[...] = mean_level
    field = joined(weight_ref, base, 0, sources, slice(0, side_x))
    out_ref[...] = chebyshev_sum(field, mean_level, cos_ref, hop_refs, row_ref)


def next_spectral_kernel(weight_ref, base, keep_ref, other_ref, last_ref, last_other_ref, cos_ref, *refs):
    hop_refs, (mean_ref, add_ref, out_ref, row_ref) = refs[:4], refs[4:]
    field = joined(weight_ref, base, 0, (keep_ref, other_ref, last_ref, last_other_ref), slice(None))
    out_ref[...] = chebyshev_sum(field, mean_ref[...], cos_ref, hop_refs, row_ref) + add_ref[...]


def pack_kernel(noise_ref, level_ref, packed_ref, damp_ref, held_ref, noise_sem, level_sem, *, scale):
    side_x = noise_ref.shape[0]
    noise_copy = pltpu.make_async_copy(noise_ref, packed_ref.at[pl.ds(0, side_x)], noise_sem)
    level_copy = pltpu.make_async_copy(level_ref, held_ref, level_sem)
    noise_copy.start()
    level_copy.start()
    level_copy.wait()
    levels = held_ref[...].astype(F32)
    damp_ref[...] = jnp.exp(-0.05 * (levels - MIDDLE))
    share = jnp.sum(levels, axis=0, keepdims=True) * scale
    packed_ref[side_x:] = jnp.broadcast_to(share, (packed_ref.shape[0] - side_x, share.shape[1]))
    noise_copy.wait()


def residual_parts(before, here, after, damp, damp_next, noise_ref, x_refs, y_refs, out_ref):
    side_x, side_y = here.shape
    half = side_x // 2
    windows = (slice(0, half), slice(half, side_x))
    y_pair = tuple(ref[:side_y] for ref in y_refs)

    def propagate(value):
        value = split(value)
        inner = [split(dot3((x_refs[0][window], x_refs[1][window]), value)) for window in windows]
        return [dot3(part, y_pair) for part in inner]

    moved = propagate(damp_next * here)
    forward_next = jnp.concatenate([after[window] - part for window, part in zip(windows, moved)], axis=0)
    moved = propagate(damp * before)
    carried = propagate(forward_next)
    for window, part, back in zip(windows, moved, carried):
        forward = here[window] - part
        out_ref[window] = noise_ref[window] - (forward - damp_next[window] * back)


def normal_kernel(
    even_ref, slices_ref, other_ref, damp_ref, damp_next_ref, noise_ref, xh_ref, xl_ref, yh_ref, yl_ref, out_ref
):
    side_y = other_ref.shape[1]
    even = even_ref[...] > 0.5
    far = slices_ref[:, :side_y]
    here = slices_ref[:, side_y:]
    near = other_ref[...]
    before = jnp.where(even, far, near)
    after = jnp.where(even, near, far)
    damps = damp_ref[...], damp_next_ref[...]
    residual_parts(before, here, after, *damps, noise_ref, (xh_ref, xl_ref), (yh_ref, yl_ref), out_ref)


def gather_kernel(*refs, outs, side_x, base):
    weight_ref, keep_ref, send_ref = refs[0], refs[-2], refs[-1]
    field_refs = refs[1:-2]
    rows_in, side_y = field_refs[0].shape
    count = len(field_refs)
    rows = 16

    def body(index, carry):
        window = pl.ds(pl.multiple_of(index * rows, rows), rows)
        fields = [ref[window, :] for ref in field_refs]
        for target, start, begin in ((keep_ref, 0, base), (send_ref, 2, base + outs * count)):
            for part in range(outs):
                place = begin + part * (count - start) - start
                total = weight_ref[place + start] * fields[start]
                for index_in in range(start + 1, count):
                    total = total + weight_ref[place + index_in] * fields[index_in]
                target[window, part * side_y : (part + 1) * side_y] = total
        return carry

    lax.fori_loop(0, side_x // rows, body, 0, unroll=4)
    if rows_in > side_x:
        extra = [ref[side_x:, :] for ref in field_refs]
        keep_ref[side_x:, :] = sum(extra)
        send_ref[side_x:, :] = sum(extra[2:])


def finish_kernel(weight_ref, base, keep_ref, other_ref, last_ref, last_other_ref, *refs):
    damp_ref, damp_next_ref, noise_ref, xh_ref, xl_ref, yh_ref, yl_ref = refs[:7]
    out_refs = refs[7:]
    sources = keep_ref, other_ref, last_ref, last_other_ref
    slices = [joined(weight_ref, base, part, sources, slice(None)) for part in range(3)]
    if len(out_refs) == 2:
        out_refs[1][...] = slices[1]
    damps = damp_ref[...], damp_next_ref[...]
    residual_parts(*slices, *damps, noise_ref, (xh_ref, xl_ref), (yh_ref, yl_ref), out_refs[0])


def basis_of(length):
    times = np.arange(length)
    phase = (2 * (times // 2)[:, None] + 1) * times[None, :] % (2 * length)
    angles = phase * (math.pi / length)
    basis = np.where((times % 2 == 0)[:, None], np.cos(angles), np.sin(angles))
    return basis, basis.T * (2.0 / length)


def times_of(inverse, slices):
    length = inverse.shape[0]
    outside = (slices < 0) | (slices >= length)
    return inverse[slices % length] * np.where(outside, -1.0, 1.0)[:, None]


def table_parts(matrix, rows):
    matrix = np.kron(matrix, np.eye(rows))
    high = matrix.astype(BF16)
    return jnp.asarray(high), jnp.asarray((matrix - high.astype(np.float64)).astype(BF16))


def ring_of(length):
    chips = length // 2
    return [*range(0, chips, 2), *reversed(range(1, chips, 2))]


def ring_pairs(length):
    path = ring_of(length)
    chips = len(path)
    pairs = []
    for place, chip in enumerate(path):
        pairs += [(2 * chip, 2 * path[(place + 1) % chips]), (2 * chip + 1, 2 * path[place - 1] + 1)]
    return pairs


def ring_weights(length, rows_of):
    path = ring_of(length)
    chips = len(path)
    reach = chips // 2
    gathers, finishes = [], []
    for device in range(length):
        core = device % 2
        place = path.index(device // 2)
        way = 1 - 2 * core
        own, partner = rows_of(device), rows_of(device ^ 1)
        arrivals = [
            2 * path[(place - way * hop) % chips] + side for hop in range(reach) for side in (core, 1 - core)
        ]
        far = 2 * path[(place + reach) % chips]
        gathers.append(np.concatenate([own[:, arrivals].ravel(), partner[:, arrivals[2:]].ravel()]))
        finishes.append(own[:, [far + core, far + 1 - core]].ravel())
    return np.stack(gathers).astype(np.float32), np.stack(finishes).astype(np.float32)


def add_partners(value, axis, step):
    count = lax.axis_size(axis)
    value = jnp.sum(value, axis=0, keepdims=True)
    shifts = range(1, min(4, count // step))
    others = [lax.ppermute(value, axis, [(i, i ^ (step * shift)) for i in range(count)]) for shift in shifts]
    return jnp.concatenate([value] + others, axis=0)


def exchange(value, axis):
    count = lax.axis_size(axis)
    rows, columns = value.shape
    blocks = value.reshape(count, rows // count, columns)
    return lax.all_to_all(blocks, axis, split_axis=0, concat_axis=0, tiled=True).reshape(rows, columns)


def by_exchange(noise, phonon_level, hops, cosine):
    side_x, side_y = noise.shape
    length = lax.axis_size("tm")
    position = lax.axis_index("tm")
    rows = side_x // length
    field_shape = shape(side_x, side_y)
    levels = phonon_level.astype(F32)
    damp = jnp.exp(-0.05 * (levels - MIDDLE))
    mean_rows = jnp.full((1, side_y), jnp.sum(levels) / (length * side_x * side_y), F32)
    basis, inverse = basis_of(length)
    forward = table_parts(basis, rows)
    times = np.arange(length)
    far = times_of(inverse, np.where(times % 2 == 0, times - 1, times + 1))
    back = [jnp.concatenate(pair, axis=0) for pair in zip(table_parts(far, rows), table_parts(inverse, rows))]

    def chebyshev(field, *operands):
        scratch = [pltpu.VMEM((16, side_y), F32)]
        return call(chebyshev_kernel, field_shape, 7 + len(operands), scratch)(field, mean_rows, cosine, *hops, *operands)

    def spectrum(field, beside):
        block = call(transform_kernel, field_shape, 3)(exchange(field, "tm"), *forward)
        block, beside = lax.optimization_barrier((block, beside))
        return exchange(block, "tm"), beside

    def residual_of(components):
        block = exchange(components, "tm")
        slices = exchange(call(transform_kernel, shape(side_x, 2 * side_y), 3)(block, *back), "tm")
        here = slices[:, side_y:]
        other = lax.ppermute(here, "tm", [(i, i ^ 1) for i in range(length)])
        even = jnp.full((1, side_y), (position % 2 == 0).astype(F32), F32)
        return here, call(normal_kernel, field_shape, 10)(even, slices, other, damp, damp_next, noise, *hops)

    power_of_two = length & (length - 1) == 0
    mean_rows = add_partners(mean_rows, "tm", 1) if power_of_two else lax.psum(mean_rows, "tm")
    field, mean_rows = spectrum(noise, mean_rows)
    step = 4
    while power_of_two and step < length:
        mean_rows = add_partners(mean_rows, "tm", step)
        step *= 4
    damp_next = lax.ppermute(damp, "tm", [(i, (i - 1) % length) for i in range(length)])
    first = chebyshev(field)
    _, second_residual = residual_of(first)
    field, _ = spectrum(second_residual, cosine)
    return residual_of(chebyshev(field, first))


def by_ring(noise, phonon_level, hops, cosine):
    side_x, side_y = noise.shape
    length = lax.axis_size("tm")
    position = lax.axis_index("tm")
    reach = length // 4
    extra = 8
    field_shape = shape(side_x, side_y)
    basis, inverse = basis_of(length)
    hop = ring_pairs(length)
    swap = [(i, i ^ 1) for i in range(length)]

    tables = [
        *ring_weights(length, lambda device: basis[device : device + 1]),
        *ring_weights(length, lambda device: times_of(inverse, np.arange(device - 1, device + 2))),
    ]
    starts = np.cumsum([0] + [table.shape[1] for table in tables]).tolist()
    forward, back = starts[:2], starts[2:4]
    table = jnp.asarray(np.concatenate(tables, axis=1))
    weights = lax.dynamic_index_in_dim(table, position, 0, keepdims=False)

    def around(own, base, outs, beside):
        partner = lax.ppermute(own, "tm", swap)
        fields = [own, partner]
        for step in range(1, reach):
            own = lax.ppermute(own, "tm", hop)
            partner = lax.ppermute(partner, "tm", hop)
            fields += [own, partner]
            if step == 1:
                own, beside = lax.optimization_barrier((own, beside))
        last = lax.ppermute(own, "tm", hop)

        def kernel(*refs):
            gather_kernel(*refs, outs=outs, side_x=side_x, base=base[0])

        wide = shape(own.shape[0], outs * side_y)
        adds = 4 * outs * len(fields) * side_x * side_y
        keep, send = call(kernel, (wide, wide), len(fields), passes=adds, scalars=1)(beside[0], *fields)
        other = lax.ppermute(send, "tm", swap)
        last_other = lax.ppermute(last, "tm", swap)
        return (beside[0], keep, other, last, last_other), beside

    def based(kernel, base):
        def run(weight_ref, *refs):
            kernel(weight_ref, base[1], *refs)

        return run

    scratch = [pltpu.VMEM((16, side_y), F32)]
    work = 12 * ORDER * 2 * side_x * side_y * max(side_x, side_y)

    def pack(*refs):
        pack_kernel(*refs, scale=1.0 / (length * side_x * side_y))

    packed, damp = pl.pallas_call(
        pack,
        out_shape=(shape(side_x + extra, side_y), field_shape),
        in_specs=[pl.BlockSpec(memory_space=pltpu.HBM)] * 2,
        out_specs=(VMEM, VMEM),
        scratch_shapes=[pltpu.VMEM((side_x, side_y), jnp.int32), pltpu.SemaphoreType.DMA, pltpu.SemaphoreType.DMA],
        compiler_params=pltpu.CompilerParams(vmem_limit_bytes=60 * 1024 * 1024),
    )(noise, phonon_level)
    parts, (weights, hops) = around(packed, forward, 1, (weights, hops))
    damp_next = lax.ppermute(damp, "tm", [(i, (i - 1) % length) for i in range(length)])
    first_kernel, next_kernel = based(first_spectral_kernel, forward), based(next_spectral_kernel, forward)
    finish = based(finish_kernel, back)
    first_outs = (field_shape, shape(1, side_y))
    first, mean_level = call(first_kernel, first_outs, 9, scratch, work, 1)(*parts, cosine, *hops)
    first, damp_next = lax.optimization_barrier((first, damp_next))
    beside = (weights,)
    parts, beside = around(first, back, 3, beside)
    (second_residual,) = call(finish, (field_shape,), 11, scalars=1)(*parts, damp, damp_next, noise, *hops)
    parts, beside = around(second_residual, forward, 1, beside)
    total = call(next_kernel, field_shape, 11, scratch, work, 1)(*parts, cosine, *hops, mean_level, first)
    parts, beside = around(total, back, 3, beside)
    residual, result = call(finish, (field_shape,) * 2, 11, scalars=1)(*parts, damp, damp_next, noise, *hops)
    return result, residual


def per_device(noise, phonon_level, hop_x, hop_y):
    _, side_x, side_y = noise.shape
    length = lax.axis_size("tm")
    position = lax.axis_index("tm")
    cosine = jnp.cos((2 * (position // 2) + 1).astype(F32) * (math.pi / length))
    cosine = jnp.full((1, side_y), cosine, F32)
    hop_parts = (shape(2 * side_x, side_x, BF16),) * 2 + (shape(2 * side_y, side_y, BF16),) * 2
    hops = call(prepare_kernel, hop_parts, 2)(hop_x, hop_y)
    ring = length % 4 == 0 and 8 <= length <= 16 and side_x % 64 == 0
    result, residual = (by_ring if ring else by_exchange)(noise[0], phonon_level[0], hops, cosine)
    return result[None], residual[None]


def solution(mesh):
    return jax.shard_map(
        per_device,
        mesh=mesh,
        in_specs=(P(("grp", "tm"), None, None), P(("grp", "tm"), None, None), P(), P()),
        out_specs=(P(("grp", "tm"), None, None), P(("grp", "tm"), None, None)),
        check_vma=False,
    )
```

```python
import math

import jax
import jax.numpy as jnp
import numpy as np
from jax import lax
from jax.experimental import pallas as pl
from jax.experimental.pallas import tpu as pltpu
from jax.sharding import PartitionSpec as P


ORDER = 10
LEVELS = 17
MIDDLE = (LEVELS - 1) // 2
BF16 = jnp.bfloat16
F32 = jnp.float32
VMEM = pl.BlockSpec(memory_space=pltpu.VMEM)


def call(kernel, out_shape, count, scratch=(), passes=0, scalars=0, out_specs=None):
    return pl.pallas_call(
        kernel,
        out_shape=out_shape,
        in_specs=[pl.BlockSpec(memory_space=pltpu.SMEM)] * scalars + [VMEM] * count,
        out_specs=out_specs or jax.tree.map(lambda _: VMEM, out_shape),
        scratch_shapes=list(scratch),
        compiler_params=pltpu.CompilerParams(vmem_limit_bytes=16 << 20),
        cost_estimate=pl.CostEstimate(flops=passes, transcendentals=0, bytes_accessed=0) if passes else None,
    )


def shape(rows, columns, kind=F32):
    return jax.ShapeDtypeStruct((rows, columns), kind)


def split(value):
    high = value.astype(BF16)
    return high, (value - high.astype(F32)).astype(BF16)


def dot3(left, right):
    def dot(a, b):
        return jnp.dot(a, b, preferred_element_type=F32)

    return dot(left[0], right[0]) + (dot(left[1], right[0]) + dot(left[0], right[1]))


def prepare_kernel(hop_x_ref, hop_y_ref, xh_ref, xl_ref, yh_ref, yl_ref):
    for ref, high_ref, low_ref in ((hop_x_ref, xh_ref, xl_ref), (hop_y_ref, yh_ref, yl_ref)):
        side = ref.shape[0]
        hop = ref[...]
        square = jnp.dot(hop, hop, precision=lax.Precision.HIGHEST, preferred_element_type=F32)
        high_ref[:side], low_ref[:side] = split(hop)
        high_ref[side:], low_ref[side:] = split(square)


def transform_kernel(block_ref, th_ref, tl_ref, out_ref):
    rows, columns = block_ref.shape
    block = split(block_ref[...])
    result = dot3((th_ref[...], tl_ref[...]), block)
    for part in range(th_ref.shape[0] // rows):
        out_ref[:, part * columns : (part + 1) * columns] = result[part * rows : (part + 1) * rows]


def chebyshev_sum(field, mean_level, cos_ref, hop_refs, weight_ref):
    xh_ref, xl_ref, yh_ref, yl_ref = hop_refs
    side_x, side_y = field.shape
    cbar = jnp.exp(-0.05 * (mean_level - MIDDLE))
    lower = 0.05
    root_lower = math.sqrt(lower)
    root_upper = 1.0 + 3.0 * cbar
    upper = root_upper * root_upper
    spread = upper - lower
    ratio = (root_upper - root_lower) / (root_upper + root_lower)
    keep = 2.0 * (2.0 - (upper + lower)) / spread
    once = -8.0 * cos_ref[...] * cbar / spread
    twice = 4.0 * cbar * cbar / spread
    weight = 2.0 / (root_upper * root_lower)
    for degree in range(ORDER + 1):
        weight_ref[degree : degree + 1, :] = weight
        weight = weight * -ratio
    half = side_x // 2

    def left(start, value):
        window = slice(start, start + half)
        return dot3((xh_ref[window], xl_ref[window]), value)

    def body(index, carry):
        ahead, second, _ = carry
        value = split(ahead)
        row = weight_ref[pl.ds(ORDER - 1 - index, 1), :]
        inner = [
            (split(left(start, value) * once), split(left(side_x + start, value) * twice)) for start in (0, half)
        ]
        parts = []
        for start, (single, double) in zip((0, half), inner):
            window = slice(start, start + half)
            hops = dot3(single, (yh_ref[:side_y], yl_ref[:side_y])) + dot3(double, (yh_ref[side_y:], yl_ref[side_y:]))
            parts.append((row * field[window] + keep * ahead[window] - second[window]) + hops)
        return jnp.concatenate(parts, axis=0), ahead, second

    ahead = weight_ref[ORDER : ORDER + 1, :] * field
    before = ahead - ahead
    result, _, second = lax.fori_loop(0, ORDER, body, (ahead, before, before), unroll=ORDER // 2)
    return 0.5 * (result - second)


def chebyshev_kernel(*refs):
    field_ref, sum_ref, cos_ref = refs[:3]
    out_ref, weight_ref = refs[-2:]
    mean_level = jnp.sum(sum_ref[...], axis=0, keepdims=True)
    total = chebyshev_sum(field_ref[...], mean_level, cos_ref, refs[3:7], weight_ref)
    out_ref[...] = total if len(refs) == 9 else total + refs[7][...]


def joined(weight_ref, base, part, refs, window):
    keep_ref, other_ref, last_ref, last_other_ref = refs
    side_y = last_ref.shape[1]
    columns = slice(part * side_y, (part + 1) * side_y)
    total = keep_ref[window, columns] + other_ref[window, columns]
    return total + (weight_ref[base + 2 * part] * last_ref[window] + weight_ref[base + 2 * part + 1] * last_other_ref[window])


def first_spectral_kernel(weight_ref, base, keep_ref, other_ref, last_ref, last_other_ref, cos_ref, *refs):
    hop_refs, (out_ref, mean_ref, row_ref) = refs[:4], refs[4:]
    side_x = out_ref.shape[0]
    sources = keep_ref, other_ref, last_ref, last_other_ref
    row = sum(ref[side_x : side_x + 1, :] for ref in sources)
    mean_level = jnp.broadcast_to(jnp.sum(row, axis=1, keepdims=True), row.shape)
    mean_ref[...] = mean_level
    field = joined(weight_ref, base, 0, sources, slice(0, side_x))
    out_ref[...] = chebyshev_sum(field, mean_level, cos_ref, hop_refs, row_ref)


def next_spectral_kernel(weight_ref, base, keep_ref, other_ref, last_ref, last_other_ref, cos_ref, *refs):
    hop_refs, (mean_ref, add_ref, out_ref, row_ref) = refs[:4], refs[4:]
    field = joined(weight_ref, base, 0, (keep_ref, other_ref, last_ref, last_other_ref), slice(None))
    out_ref[...] = chebyshev_sum(field, mean_ref[...], cos_ref, hop_refs, row_ref) + add_ref[...]


def pack_kernel(noise_ref, level_ref, packed_ref, damp_ref, held_ref, noise_sem, level_sem, *, scale):
    side_x = noise_ref.shape[0]
    noise_copy = pltpu.make_async_copy(noise_ref, packed_ref.at[pl.ds(0, side_x)], noise_sem)
    level_copy = pltpu.make_async_copy(level_ref, held_ref, level_sem)
    noise_copy.start()
    level_copy.start()
    level_copy.wait()
    levels = held_ref[...].astype(F32)
    damp_ref[...] = jnp.exp(-0.05 * (levels - MIDDLE))
    share = jnp.sum(levels, axis=0, keepdims=True) * scale
    packed_ref[side_x:] = jnp.broadcast_to(share, (packed_ref.shape[0] - side_x, share.shape[1]))
    noise_copy.wait()


def residual_parts(before, here, after, damp, damp_next, noise_ref, x_refs, y_refs, out_ref, written=None):
    side_x, side_y = here.shape
    half = side_x // 2
    windows = (slice(0, half), slice(half, side_x))
    y_pair = tuple(ref[:side_y] for ref in y_refs)

    def propagate(value):
        value = split(value)
        inner = [split(dot3((x_refs[0][window], x_refs[1][window]), value)) for window in windows]
        return [dot3(part, y_pair) for part in inner]

    moved = propagate(damp_next * here)
    forward_next = jnp.concatenate([after[window] - part for window, part in zip(windows, moved)], axis=0)
    moved = propagate(damp * before)
    carried = propagate(forward_next)
    for window, part, back in zip(windows, moved, carried):
        forward = here[window] - part
        out_ref[window] = noise_ref[window] - (forward - damp_next[window] * back)
        if written is not None:
            written(window)


def normal_kernel(
    even_ref, slices_ref, other_ref, damp_ref, damp_next_ref, noise_ref, xh_ref, xl_ref, yh_ref, yl_ref, out_ref
):
    side_y = other_ref.shape[1]
    even = even_ref[...] > 0.5
    far = slices_ref[:, :side_y]
    here = slices_ref[:, side_y:]
    near = other_ref[...]
    before = jnp.where(even, far, near)
    after = jnp.where(even, near, far)
    damps = damp_ref[...], damp_next_ref[...]
    residual_parts(before, here, after, *damps, noise_ref, (xh_ref, xl_ref), (yh_ref, yl_ref), out_ref)


def gather_kernel(*refs, outs, side_x, base):
    weight_ref, keep_ref, send_ref = refs[0], refs[-2], refs[-1]
    field_refs = refs[1:-2]
    rows_in, side_y = field_refs[0].shape
    count = len(field_refs)
    rows = 16

    def body(index, carry):
        window = pl.ds(pl.multiple_of(index * rows, rows), rows)
        fields = [ref[window, :] for ref in field_refs]
        for target, start, begin in ((keep_ref, 0, base), (send_ref, 2, base + outs * count)):
            for part in range(outs):
                place = begin + part * (count - start) - start
                total = weight_ref[place + start] * fields[start]
                for index_in in range(start + 1, count):
                    total = total + weight_ref[place + index_in] * fields[index_in]
                target[window, part * side_y : (part + 1) * side_y] = total
        return carry

    lax.fori_loop(0, side_x // rows, body, 0, unroll=4)
    if rows_in > side_x:
        extra = [ref[side_x:, :] for ref in field_refs]
        keep_ref[side_x:, :] = sum(extra)
        send_ref[side_x:, :] = sum(extra[2:])


def finish_kernel(weight_ref, base, keep_ref, other_ref, last_ref, last_other_ref, *refs):
    damp_ref, damp_next_ref, noise_ref, xh_ref, xl_ref, yh_ref, yl_ref = refs[:7]
    out_refs = refs[7:]
    sources = keep_ref, other_ref, last_ref, last_other_ref
    slices = [joined(weight_ref, base, part, sources, slice(None)) for part in range(3)]
    copies = []
    out_ref = out_refs[0]

    def send(source, target, place):
        copies.append(pltpu.make_async_copy(source, target, out_refs[-1].at[place]))
        copies[-1].start()

    written = None
    if len(out_refs) > 1:
        residual_ref, result_ref, out_ref, held_ref = out_refs[:4]
        held_ref[...] = slices[1]
        send(held_ref, result_ref, 0)

        def written(window):
            send(out_ref.at[window], residual_ref.at[window], len(copies))

    damps = damp_ref[...], damp_next_ref[...]
    residual_parts(*slices, *damps, noise_ref, (xh_ref, xl_ref), (yh_ref, yl_ref), out_ref, written)
    for copy in copies:
        copy.wait()


def basis_of(length):
    times = np.arange(length)
    phase = (2 * (times // 2)[:, None] + 1) * times[None, :] % (2 * length)
    angles = phase * (math.pi / length)
    basis = np.where((times % 2 == 0)[:, None], np.cos(angles), np.sin(angles))
    return basis, basis.T * (2.0 / length)


def times_of(inverse, slices):
    length = inverse.shape[0]
    outside = (slices < 0) | (slices >= length)
    return inverse[slices % length] * np.where(outside, -1.0, 1.0)[:, None]


def table_parts(matrix, rows):
    matrix = np.kron(matrix, np.eye(rows))
    high = matrix.astype(BF16)
    return jnp.asarray(high), jnp.asarray((matrix - high.astype(np.float64)).astype(BF16))


def ring_of(length):
    chips = length // 2
    return [*range(0, chips, 2), *reversed(range(1, chips, 2))]


def ring_pairs(length):
    path = ring_of(length)
    chips = len(path)
    pairs = []
    for place, chip in enumerate(path):
        pairs += [(2 * chip, 2 * path[(place + 1) % chips]), (2 * chip + 1, 2 * path[place - 1] + 1)]
    return pairs


def ring_weights(length, rows_of):
    path = ring_of(length)
    chips = len(path)
    reach = chips // 2
    gathers, finishes = [], []
    for device in range(length):
        core = device % 2
        place = path.index(device // 2)
        way = 1 - 2 * core
        own, partner = rows_of(device), rows_of(device ^ 1)
        arrivals = [
            2 * path[(place - way * hop) % chips] + side for hop in range(reach) for side in (core, 1 - core)
        ]
        far = 2 * path[(place + reach) % chips]
        gathers.append(np.concatenate([own[:, arrivals].ravel(), partner[:, arrivals[2:]].ravel()]))
        finishes.append(own[:, [far + core, far + 1 - core]].ravel())
    return np.stack(gathers).astype(np.float32), np.stack(finishes).astype(np.float32)


def add_partners(value, axis, step):
    count = lax.axis_size(axis)
    value = jnp.sum(value, axis=0, keepdims=True)
    shifts = range(1, min(4, count // step))
    others = [lax.ppermute(value, axis, [(i, i ^ (step * shift)) for i in range(count)]) for shift in shifts]
    return jnp.concatenate([value] + others, axis=0)


def exchange(value, axis):
    count = lax.axis_size(axis)
    rows, columns = value.shape
    blocks = value.reshape(count, rows // count, columns)
    return lax.all_to_all(blocks, axis, split_axis=0, concat_axis=0, tiled=True).reshape(rows, columns)


def by_exchange(noise, phonon_level, hops, cosine):
    side_x, side_y = noise.shape
    length = lax.axis_size("tm")
    position = lax.axis_index("tm")
    rows = side_x // length
    field_shape = shape(side_x, side_y)
    levels = phonon_level.astype(F32)
    damp = jnp.exp(-0.05 * (levels - MIDDLE))
    mean_rows = jnp.full((1, side_y), jnp.sum(levels) / (length * side_x * side_y), F32)
    basis, inverse = basis_of(length)
    forward = table_parts(basis, rows)
    times = np.arange(length)
    far = times_of(inverse, np.where(times % 2 == 0, times - 1, times + 1))
    back = [jnp.concatenate(pair, axis=0) for pair in zip(table_parts(far, rows), table_parts(inverse, rows))]

    def chebyshev(field, *operands):
        scratch = [pltpu.VMEM((16, side_y), F32)]
        return call(chebyshev_kernel, field_shape, 7 + len(operands), scratch)(field, mean_rows, cosine, *hops, *operands)

    def spectrum(field, beside):
        block = call(transform_kernel, field_shape, 3)(exchange(field, "tm"), *forward)
        block, beside = lax.optimization_barrier((block, beside))
        return exchange(block, "tm"), beside

    def residual_of(components):
        block = exchange(components, "tm")
        slices = exchange(call(transform_kernel, shape(side_x, 2 * side_y), 3)(block, *back), "tm")
        here = slices[:, side_y:]
        other = lax.ppermute(here, "tm", [(i, i ^ 1) for i in range(length)])
        even = jnp.full((1, side_y), (position % 2 == 0).astype(F32), F32)
        return here, call(normal_kernel, field_shape, 10)(even, slices, other, damp, damp_next, noise, *hops)

    power_of_two = length & (length - 1) == 0
    mean_rows = add_partners(mean_rows, "tm", 1) if power_of_two else lax.psum(mean_rows, "tm")
    field, mean_rows = spectrum(noise, mean_rows)
    step = 4
    while power_of_two and step < length:
        mean_rows = add_partners(mean_rows, "tm", step)
        step *= 4
    damp_next = lax.ppermute(damp, "tm", [(i, (i - 1) % length) for i in range(length)])
    first = chebyshev(field)
    _, second_residual = residual_of(first)
    field, _ = spectrum(second_residual, cosine)
    return residual_of(chebyshev(field, first))


def by_ring(noise, phonon_level, hops, cosine):
    side_x, side_y = noise.shape
    length = lax.axis_size("tm")
    position = lax.axis_index("tm")
    reach = length // 4
    extra = 8
    field_shape = shape(side_x, side_y)
    basis, inverse = basis_of(length)
    hop = ring_pairs(length)
    swap = [(i, i ^ 1) for i in range(length)]

    tables = [
        *ring_weights(length, lambda device: basis[device : device + 1]),
        *ring_weights(length, lambda device: times_of(inverse, np.arange(device - 1, device + 2))),
    ]
    starts = np.cumsum([0] + [table.shape[1] for table in tables]).tolist()
    forward, back = starts[:2], starts[2:4]
    table = jnp.asarray(np.concatenate(tables, axis=1))
    weights = lax.dynamic_index_in_dim(table, position, 0, keepdims=False)

    def around(own, base, outs, beside):
        partner = lax.ppermute(own, "tm", swap)
        fields = [own, partner]
        for step in range(1, reach):
            own = lax.ppermute(own, "tm", hop)
            partner = lax.ppermute(partner, "tm", hop)
            fields += [own, partner]
            if step == 1:
                own, beside = lax.optimization_barrier((own, beside))
        last = lax.ppermute(own, "tm", hop)

        def kernel(*refs):
            gather_kernel(*refs, outs=outs, side_x=side_x, base=base[0])

        wide = shape(own.shape[0], outs * side_y)
        adds = 4 * outs * len(fields) * side_x * side_y
        keep, send = call(kernel, (wide, wide), len(fields), passes=adds, scalars=1)(beside[0], *fields)
        other = lax.ppermute(send, "tm", swap)
        last_other = lax.ppermute(last, "tm", swap)
        return (beside[0], keep, other, last, last_other), beside

    def based(kernel, base):
        def run(weight_ref, *refs):
            kernel(weight_ref, base[1], *refs)

        return run

    scratch = [pltpu.VMEM((16, side_y), F32)]
    work = 12 * ORDER * 2 * side_x * side_y * max(side_x, side_y)

    def pack(*refs):
        pack_kernel(*refs, scale=1.0 / (length * side_x * side_y))

    packed, damp = pl.pallas_call(
        pack,
        out_shape=(shape(side_x + extra, side_y), field_shape),
        in_specs=[pl.BlockSpec(memory_space=pltpu.HBM)] * 2,
        out_specs=(VMEM, VMEM),
        scratch_shapes=[pltpu.VMEM((side_x, side_y), jnp.int32), pltpu.SemaphoreType.DMA, pltpu.SemaphoreType.DMA],
        compiler_params=pltpu.CompilerParams(vmem_limit_bytes=60 * 1024 * 1024),
    )(noise, phonon_level)
    parts, (weights, hops) = around(packed, forward, 1, (weights, hops))
    damp_wrap = lax.ppermute(damp, "tm", [(0, length - 1)])
    damp_next = lax.ppermute(damp, "tm", [(i, i - 1) for i in range(1, length)])
    first_kernel, next_kernel = based(first_spectral_kernel, forward), based(next_spectral_kernel, forward)
    finish = based(finish_kernel, back)
    first_outs = (field_shape, shape(1, side_y))
    first, mean_level = call(first_kernel, first_outs, 9, scratch, work, 1)(*parts, cosine, *hops)
    first, damp_next, damp_wrap = lax.optimization_barrier((first, damp_next, damp_wrap))
    damp_next = damp_next + damp_wrap
    beside = (weights,)
    parts, beside = around(first, back, 3, beside)
    (second_residual,) = call(finish, (field_shape,), 11, scalars=1)(*parts, damp, damp_next, noise, *hops)
    parts, beside = around(second_residual, forward, 1, beside)
    total = call(next_kernel, field_shape, 11, scratch, work, 1)(*parts, cosine, *hops, mean_level, first)
    parts, beside = around(total, back, 3, beside)
    scratch = [pltpu.VMEM((side_x, side_y), F32)] * 2 + [pltpu.SemaphoreType.DMA((3,))]
    out_specs = (pl.BlockSpec(memory_space=pltpu.HBM),) * 2
    last_finish = call(finish, (field_shape,) * 2, 11, scratch, scalars=1, out_specs=out_specs)
    residual, result = last_finish(*parts, damp, damp_next, noise, *hops)
    return result, residual


def per_device(noise, phonon_level, hop_x, hop_y):
    _, side_x, side_y = noise.shape
    length = lax.axis_size("tm")
    position = lax.axis_index("tm")
    cosine = jnp.cos((2 * (position // 2) + 1).astype(F32) * (math.pi / length))
    cosine = jnp.full((1, side_y), cosine, F32)
    hop_parts = (shape(2 * side_x, side_x, BF16),) * 2 + (shape(2 * side_y, side_y, BF16),) * 2
    hops = call(prepare_kernel, hop_parts, 2)(hop_x, hop_y)
    ring = length % 4 == 0 and 8 <= length <= 16 and side_x % 64 == 0
    result, residual = (by_ring if ring else by_exchange)(noise[0], phonon_level[0], hops, cosine)
    return result[None], residual[None]


def solution(mesh):
    return jax.shard_map(
        per_device,
        mesh=mesh,
        in_specs=(P(("grp", "tm"), None, None), P(("grp", "tm"), None, None), P(), P()),
        out_specs=(P(("grp", "tm"), None, None), P(("grp", "tm"), None, None)),
        check_vma=False,
    )
```

```python
import math

import jax
import jax.numpy as jnp
import numpy as np
from jax import lax
from jax.experimental import pallas as pl
from jax.experimental.pallas import tpu as pltpu
from jax.sharding import PartitionSpec as P


ORDER = 10
LEVELS = 17
MIDDLE = (LEVELS - 1) // 2
BF16 = jnp.bfloat16
F32 = jnp.float32
VMEM = pl.BlockSpec(memory_space=pltpu.VMEM)


def call(kernel, out_shape, count, scratch=(), passes=0, scalars=0):
    return pl.pallas_call(
        kernel,
        out_shape=out_shape,
        in_specs=[pl.BlockSpec(memory_space=pltpu.SMEM)] * scalars + [VMEM] * count,
        out_specs=jax.tree.map(lambda _: VMEM, out_shape),
        scratch_shapes=list(scratch),
        compiler_params=pltpu.CompilerParams(vmem_limit_bytes=16 << 20),
        cost_estimate=pl.CostEstimate(flops=passes, transcendentals=0, bytes_accessed=0) if passes else None,
    )


def shape(rows, columns, kind=F32):
    return jax.ShapeDtypeStruct((rows, columns), kind)


def split(value):
    high = value.astype(BF16)
    return high, (value - high.astype(F32)).astype(BF16)


def dot3(left, right):
    def dot(a, b):
        return jnp.dot(a, b, preferred_element_type=F32)

    return dot(left[0], right[0]) + (dot(left[1], right[0]) + dot(left[0], right[1]))


def prepare_kernel(hop_x_ref, hop_y_ref, xh_ref, xl_ref, yh_ref, yl_ref):
    for ref, high_ref, low_ref in ((hop_x_ref, xh_ref, xl_ref), (hop_y_ref, yh_ref, yl_ref)):
        side = ref.shape[0]
        hop = ref[...]
        square = jnp.dot(hop, hop, precision=lax.Precision.HIGHEST, preferred_element_type=F32)
        high_ref[:side], low_ref[:side] = split(hop)
        high_ref[side:], low_ref[side:] = split(square)


def transform_kernel(block_ref, th_ref, tl_ref, out_ref):
    rows, columns = block_ref.shape
    block = split(block_ref[...])
    result = dot3((th_ref[...], tl_ref[...]), block)
    for part in range(th_ref.shape[0] // rows):
        out_ref[:, part * columns : (part + 1) * columns] = result[part * rows : (part + 1) * rows]


def chebyshev_sum(field, mean_level, cos_ref, hop_refs, weight_ref):
    xh_ref, xl_ref, yh_ref, yl_ref = hop_refs
    side_x, side_y = field.shape
    cbar = jnp.exp(-0.05 * (mean_level - MIDDLE))
    lower = 0.05
    root_lower = math.sqrt(lower)
    root_upper = 1.0 + 3.0 * cbar
    upper = root_upper * root_upper
    spread = upper - lower
    ratio = (root_upper - root_lower) / (root_upper + root_lower)
    keep = 2.0 * (2.0 - (upper + lower)) / spread
    once = -8.0 * cos_ref[...] * cbar / spread
    twice = 4.0 * cbar * cbar / spread
    weight = 2.0 / (root_upper * root_lower)
    for degree in range(ORDER + 1):
        weight_ref[degree : degree + 1, :] = weight
        weight = weight * -ratio
    half = side_x // 2

    def left(start, value):
        window = slice(start, start + half)
        return dot3((xh_ref[window], xl_ref[window]), value)

    def body(index, carry):
        ahead, second, _ = carry
        value = split(ahead)
        row = weight_ref[pl.ds(ORDER - 1 - index, 1), :]
        inner = [
            (split(left(start, value) * once), split(left(side_x + start, value) * twice)) for start in (0, half)
        ]
        parts = []
        for start, (single, double) in zip((0, half), inner):
            window = slice(start, start + half)
            hops = dot3(single, (yh_ref[:side_y], yl_ref[:side_y])) + dot3(double, (yh_ref[side_y:], yl_ref[side_y:]))
            parts.append((row * field[window] + keep * ahead[window] - second[window]) + hops)
        return jnp.concatenate(parts, axis=0), ahead, second

    ahead = weight_ref[ORDER : ORDER + 1, :] * field
    before = ahead - ahead
    result, _, second = lax.fori_loop(0, ORDER, body, (ahead, before, before), unroll=True)
    return 0.5 * (result - second)


def chebyshev_kernel(*refs):
    field_ref, sum_ref, cos_ref = refs[:3]
    out_ref, weight_ref = refs[-2:]
    mean_level = jnp.sum(sum_ref[...], axis=0, keepdims=True)
    total = chebyshev_sum(field_ref[...], mean_level, cos_ref, refs[3:7], weight_ref)
    out_ref[...] = total if len(refs) == 9 else total + refs[7][...]


def joined(weight_ref, base, part, refs, window):
    keep_ref, other_ref, last_ref, last_other_ref = refs
    side_y = last_ref.shape[1]
    columns = slice(part * side_y, (part + 1) * side_y)
    total = keep_ref[window, columns] + other_ref[window, columns]
    return total + (weight_ref[base + 2 * part] * last_ref[window] + weight_ref[base + 2 * part + 1] * last_other_ref[window])


def first_spectral_kernel(weight_ref, base, keep_ref, other_ref, last_ref, last_other_ref, cos_ref, *refs):
    hop_refs, (out_ref, mean_ref, row_ref) = refs[:4], refs[4:]
    side_x = out_ref.shape[0]
    sources = keep_ref, other_ref, last_ref, last_other_ref
    row = sum(ref[side_x : side_x + 1, :] for ref in sources)
    mean_level = jnp.broadcast_to(jnp.sum(row, axis=1, keepdims=True), row.shape)
    mean_ref[...] = mean_level
    field = joined(weight_ref, base, 0, sources, slice(0, side_x))
    out_ref[...] = chebyshev_sum(field, mean_level, cos_ref, hop_refs, row_ref)


def pack_kernel(noise_ref, level_ref, packed_ref, damp_ref, held_ref, noise_sem, level_sem, *, scale):
    side_x = noise_ref.shape[0]
    noise_copy = pltpu.make_async_copy(noise_ref, packed_ref.at[pl.ds(0, side_x)], noise_sem)
    level_copy = pltpu.make_async_copy(level_ref, held_ref, level_sem)
    noise_copy.start()
    level_copy.start()
    level_copy.wait()
    levels = held_ref[...].astype(F32)
    damp_ref[...] = jnp.exp(-0.05 * (levels - MIDDLE))
    share = jnp.sum(levels, axis=0, keepdims=True) * scale
    packed_ref[side_x:] = jnp.broadcast_to(share, (packed_ref.shape[0] - side_x, share.shape[1]))
    noise_copy.wait()


def residual_parts(before, here, after, damp, damp_next, noise_ref, x_refs, y_refs, out_ref):
    side_x, side_y = here.shape
    half = side_x // 2
    windows = (slice(0, half), slice(half, side_x))
    y_pair = tuple(ref[:side_y] for ref in y_refs)

    def propagate(value):
        value = split(value)
        inner = [split(dot3((x_refs[0][window], x_refs[1][window]), value)) for window in windows]
        return [dot3(part, y_pair) for part in inner]

    moved = propagate(damp_next * here)
    forward_next = jnp.concatenate([after[window] - part for window, part in zip(windows, moved)], axis=0)
    moved = propagate(damp * before)
    carried = propagate(forward_next)
    for window, part, back in zip(windows, moved, carried):
        forward = here[window] - part
        out_ref[window] = noise_ref[window] - (forward - damp_next[window] * back)


def normal_kernel(
    even_ref, slices_ref, other_ref, damp_ref, damp_next_ref, noise_ref, xh_ref, xl_ref, yh_ref, yl_ref, out_ref
):
    side_y = other_ref.shape[1]
    even = even_ref[...] > 0.5
    far = slices_ref[:, :side_y]
    here = slices_ref[:, side_y:]
    near = other_ref[...]
    before = jnp.where(even, far, near)
    after = jnp.where(even, near, far)
    damps = damp_ref[...], damp_next_ref[...]
    residual_parts(before, here, after, *damps, noise_ref, (xh_ref, xl_ref), (yh_ref, yl_ref), out_ref)


def gather_kernel(*refs, outs, side_x, base):
    weight_ref, keep_ref, send_ref = refs[0], refs[-2], refs[-1]
    field_refs = refs[1:-2]
    rows_in, side_y = field_refs[0].shape
    count = len(field_refs)
    rows = 16

    def body(index, carry):
        window = pl.ds(pl.multiple_of(index * rows, rows), rows)
        fields = [ref[window, :] for ref in field_refs]
        for target, start, begin in ((keep_ref, 0, base), (send_ref, 2, base + outs * count)):
            for part in range(outs):
                place = begin + part * (count - start) - start
                total = weight_ref[place + start] * fields[start]
                for index_in in range(start + 1, count):
                    total = total + weight_ref[place + index_in] * fields[index_in]
                target[window, part * side_y : (part + 1) * side_y] = total
        return carry

    lax.fori_loop(0, side_x // rows, body, 0, unroll=4)
    if rows_in > side_x:
        extra = [ref[side_x:, :] for ref in field_refs]
        keep_ref[side_x:, :] = sum(extra)
        send_ref[side_x:, :] = sum(extra[2:])


def finish_kernel(weight_ref, base, keep_ref, other_ref, last_ref, last_other_ref, *refs):
    damp_ref, damp_next_ref, noise_ref, xh_ref, xl_ref, yh_ref, yl_ref = refs[:7]
    out_refs = refs[7:]
    sources = keep_ref, other_ref, last_ref, last_other_ref
    slices = [joined(weight_ref, base, part, sources, slice(None)) for part in range(3)]
    if len(out_refs) == 2:
        out_refs[1][...] = slices[1]
    damps = damp_ref[...], damp_next_ref[...]
    residual_parts(*slices, *damps, noise_ref, (xh_ref, xl_ref), (yh_ref, yl_ref), out_refs[0])


def basis_of(length):
    times = np.arange(length)
    phase = (2 * (times // 2)[:, None] + 1) * times[None, :] % (2 * length)
    angles = phase * (math.pi / length)
    basis = np.where((times % 2 == 0)[:, None], np.cos(angles), np.sin(angles))
    return basis, basis.T * (2.0 / length)


def times_of(inverse, slices):
    length = inverse.shape[0]
    outside = (slices < 0) | (slices >= length)
    return inverse[slices % length] * np.where(outside, -1.0, 1.0)[:, None]


def table_parts(matrix, rows):
    matrix = np.kron(matrix, np.eye(rows))
    high = matrix.astype(BF16)
    return jnp.asarray(high), jnp.asarray((matrix - high.astype(np.float64)).astype(BF16))


def ring_of(length):
    chips = length // 2
    return [*range(0, chips, 2), *reversed(range(1, chips, 2))]


def ring_pairs(length):
    path = ring_of(length)
    chips = len(path)
    pairs = []
    for place, chip in enumerate(path):
        pairs += [(2 * chip, 2 * path[(place + 1) % chips]), (2 * chip + 1, 2 * path[place - 1] + 1)]
    return pairs


def ring_weights(length, rows_of):
    path = ring_of(length)
    chips = len(path)
    reach = chips // 2
    gathers, finishes = [], []
    for device in range(length):
        core = device % 2
        place = path.index(device // 2)
        way = 1 - 2 * core
        own, partner = rows_of(device), rows_of(device ^ 1)
        arrivals = [
            2 * path[(place - way * hop) % chips] + side for hop in range(reach) for side in (core, 1 - core)
        ]
        far = 2 * path[(place + reach) % chips]
        gathers.append(np.concatenate([own[:, arrivals].ravel(), partner[:, arrivals[2:]].ravel()]))
        finishes.append(own[:, [far + core, far + 1 - core]].ravel())
    return np.stack(gathers).astype(np.float32), np.stack(finishes).astype(np.float32)


def add_partners(value, axis, step):
    count = lax.axis_size(axis)
    value = jnp.sum(value, axis=0, keepdims=True)
    shifts = range(1, min(4, count // step))
    others = [lax.ppermute(value, axis, [(i, i ^ (step * shift)) for i in range(count)]) for shift in shifts]
    return jnp.concatenate([value] + others, axis=0)


def exchange(value, axis):
    count = lax.axis_size(axis)
    rows, columns = value.shape
    blocks = value.reshape(count, rows // count, columns)
    return lax.all_to_all(blocks, axis, split_axis=0, concat_axis=0, tiled=True).reshape(rows, columns)


def by_exchange(noise, phonon_level, hops, cosine):
    side_x, side_y = noise.shape
    length = lax.axis_size("tm")
    position = lax.axis_index("tm")
    rows = side_x // length
    field_shape = shape(side_x, side_y)
    levels = phonon_level.astype(F32)
    damp = jnp.exp(-0.05 * (levels - MIDDLE))
    mean_rows = jnp.full((1, side_y), jnp.sum(levels) / (length * side_x * side_y), F32)
    basis, inverse = basis_of(length)
    forward = table_parts(basis, rows)
    times = np.arange(length)
    far = times_of(inverse, np.where(times % 2 == 0, times - 1, times + 1))
    back = [jnp.concatenate(pair, axis=0) for pair in zip(table_parts(far, rows), table_parts(inverse, rows))]

    def chebyshev(field, *operands):
        scratch = [pltpu.VMEM((16, side_y), F32)]
        return call(chebyshev_kernel, field_shape, 7 + len(operands), scratch)(field, mean_rows, cosine, *hops, *operands)

    def spectrum(field, beside):
        block = call(transform_kernel, field_shape, 3)(exchange(field, "tm"), *forward)
        block, beside = lax.optimization_barrier((block, beside))
        return exchange(block, "tm"), beside

    def residual_of(components):
        block = exchange(components, "tm")
        slices = exchange(call(transform_kernel, shape(side_x, 2 * side_y), 3)(block, *back), "tm")
        here = slices[:, side_y:]
        other = lax.ppermute(here, "tm", [(i, i ^ 1) for i in range(length)])
        even = jnp.full((1, side_y), (position % 2 == 0).astype(F32), F32)
        return here, call(normal_kernel, field_shape, 10)(even, slices, other, damp, damp_next, noise, *hops)

    power_of_two = length & (length - 1) == 0
    mean_rows = add_partners(mean_rows, "tm", 1) if power_of_two else lax.psum(mean_rows, "tm")
    field, mean_rows = spectrum(noise, mean_rows)
    step = 4
    while power_of_two and step < length:
        mean_rows = add_partners(mean_rows, "tm", step)
        step *= 4
    damp_next = lax.ppermute(damp, "tm", [(i, (i - 1) % length) for i in range(length)])
    first = chebyshev(field)
    _, second_residual = residual_of(first)
    field, _ = spectrum(second_residual, cosine)
    return residual_of(chebyshev(field, first))


def by_ring(noise, phonon_level, hops, cosine):
    side_x, side_y = noise.shape
    length = lax.axis_size("tm")
    position = lax.axis_index("tm")
    reach = length // 4
    extra = 8
    field_shape = shape(side_x, side_y)
    basis, inverse = basis_of(length)
    hop = ring_pairs(length)
    swap = [(i, i ^ 1) for i in range(length)]

    tables = [
        *ring_weights(length, lambda device: basis[device : device + 1]),
        *ring_weights(length, lambda device: times_of(inverse, np.arange(device - 1, device + 2))),
    ]
    starts = np.cumsum([0] + [table.shape[1] for table in tables]).tolist()
    forward, back = starts[:2], starts[2:4]
    table = jnp.asarray(np.concatenate(tables, axis=1))
    weights = lax.dynamic_index_in_dim(table, position, 0, keepdims=False)

    def around(own, base, outs, beside):
        partner = lax.ppermute(own, "tm", swap)
        fields = [own, partner]
        for step in range(1, reach):
            own = lax.ppermute(own, "tm", hop)
            partner = lax.ppermute(partner, "tm", hop)
            fields += [own, partner]
            if step == 1:
                own, beside = lax.optimization_barrier((own, beside))
        last = lax.ppermute(own, "tm", hop)

        def kernel(*refs):
            gather_kernel(*refs, outs=outs, side_x=side_x, base=base[0])

        wide = shape(own.shape[0], outs * side_y)
        adds = 4 * outs * len(fields) * side_x * side_y
        keep, send = call(kernel, (wide, wide), len(fields), passes=adds, scalars=1)(beside[0], *fields)
        other = lax.ppermute(send, "tm", swap)
        last_other = lax.ppermute(last, "tm", swap)
        return (beside[0], keep, other, last, last_other), beside

    def based(kernel, base):
        def run(weight_ref, *refs):
            kernel(weight_ref, base[1], *refs)

        return run

    scratch = [pltpu.VMEM((16, side_y), F32)]
    work = 12 * ORDER * 2 * side_x * side_y * max(side_x, side_y)

    def pack(*refs):
        pack_kernel(*refs, scale=1.0 / (length * side_x * side_y))

    packed, damp = pl.pallas_call(
        pack,
        out_shape=(shape(side_x + extra, side_y), field_shape),
        in_specs=[pl.BlockSpec(memory_space=pltpu.HBM)] * 2,
        out_specs=(VMEM, VMEM),
        scratch_shapes=[pltpu.VMEM((side_x, side_y), jnp.int32), pltpu.SemaphoreType.DMA, pltpu.SemaphoreType.DMA],
        compiler_params=pltpu.CompilerParams(vmem_limit_bytes=60 * 1024 * 1024),
    )(noise, phonon_level)
    parts, (weights, hops) = around(packed, forward, 1, (weights, hops))
    damp_next = lax.ppermute(damp, "tm", [(i, (i - 1) % length) for i in range(length)])
    first_kernel = based(first_spectral_kernel, forward)
    finish = based(finish_kernel, back)
    first_outs = (field_shape, shape(1, side_y))
    first, mean_level = call(first_kernel, first_outs, 9, scratch, work, 1)(*parts, cosine, *hops)
    first, damp_next = lax.optimization_barrier((first, damp_next))
    beside = (weights,)
    parts, beside = around(first, back, 3, beside)
    (second_residual,) = call(finish, (field_shape,), 11, scalars=1)(*parts, damp, damp_next, noise, *hops)
    field_table = table_parts(basis, side_x // length)
    field = exchange(call(transform_kernel, field_shape, 3)(exchange(second_residual, "tm"), *field_table), "tm")
    total = call(chebyshev_kernel, field_shape, 8, scratch, work)(field, mean_level, cosine, *hops, first)
    parts, beside = around(total, back, 3, beside)
    residual, result = call(finish, (field_shape,) * 2, 11, scalars=1)(*parts, damp, damp_next, noise, *hops)
    return result, residual


def per_device(noise, phonon_level, hop_x, hop_y):
    _, side_x, side_y = noise.shape
    length = lax.axis_size("tm")
    position = lax.axis_index("tm")
    cosine = jnp.cos((2 * (position // 2) + 1).astype(F32) * (math.pi / length))
    cosine = jnp.full((1, side_y), cosine, F32)
    hop_parts = (shape(2 * side_x, side_x, BF16),) * 2 + (shape(2 * side_y, side_y, BF16),) * 2
    hops = call(prepare_kernel, hop_parts, 2)(hop_x, hop_y)
    ring = length % 4 == 0 and 8 <= length <= 16 and side_x % 64 == 0
    result, residual = (by_ring if ring else by_exchange)(noise[0], phonon_level[0], hops, cosine)
    return result[None], residual[None]


def solution(mesh):
    return jax.shard_map(
        per_device,
        mesh=mesh,
        in_specs=(P(("grp", "tm"), None, None), P(("grp", "tm"), None, None), P(), P()),
        out_specs=(P(("grp", "tm"), None, None), P(("grp", "tm"), None, None)),
        check_vma=False,
    )
```

```python
import math

import jax
import jax.numpy as jnp
import numpy as np
from jax import lax
from jax.experimental import pallas as pl
from jax.experimental.pallas import tpu as pltpu
from jax.sharding import PartitionSpec as P


ORDER = 10
LEVELS = 17
MIDDLE = (LEVELS - 1) // 2
BF16 = jnp.bfloat16
F32 = jnp.float32
VMEM = pl.BlockSpec(memory_space=pltpu.VMEM)


def call(kernel, out_shape, count, scratch=(), passes=0, scalars=0):
    return pl.pallas_call(
        kernel,
        out_shape=out_shape,
        in_specs=[pl.BlockSpec(memory_space=pltpu.SMEM)] * scalars + [VMEM] * count,
        out_specs=jax.tree.map(lambda _: VMEM, out_shape),
        scratch_shapes=list(scratch),
        compiler_params=pltpu.CompilerParams(vmem_limit_bytes=16 << 20),
        cost_estimate=pl.CostEstimate(flops=passes, transcendentals=0, bytes_accessed=0) if passes else None,
    )


def shape(rows, columns, kind=F32):
    return jax.ShapeDtypeStruct((rows, columns), kind)


def split(value):
    high = value.astype(BF16)
    return high, (value - high.astype(F32)).astype(BF16)


def dot3(left, right):
    def dot(a, b):
        return jnp.dot(a, b, preferred_element_type=F32)

    return dot(left[0], right[0]) + (dot(left[1], right[0]) + dot(left[0], right[1]))


def prepare_kernel(hop_x_ref, hop_y_ref, xh_ref, xl_ref, yh_ref, yl_ref):
    for ref, high_ref, low_ref in ((hop_x_ref, xh_ref, xl_ref), (hop_y_ref, yh_ref, yl_ref)):
        side = ref.shape[0]
        hop = ref[...]
        square = jnp.dot(hop, hop, precision=lax.Precision.HIGHEST, preferred_element_type=F32)
        high_ref[:side], low_ref[:side] = split(hop)
        high_ref[side:], low_ref[side:] = split(square)


def transform_kernel(block_ref, th_ref, tl_ref, out_ref):
    rows, columns = block_ref.shape
    block = split(block_ref[...])
    result = dot3((th_ref[...], tl_ref[...]), block)
    for part in range(th_ref.shape[0] // rows):
        out_ref[:, part * columns : (part + 1) * columns] = result[part * rows : (part + 1) * rows]


def chebyshev_sum(field, mean_level, cos_ref, hop_refs, weight_ref):
    xh_ref, xl_ref, yh_ref, yl_ref = hop_refs
    side_x, side_y = field.shape
    cbar = jnp.exp(-0.05 * (mean_level - MIDDLE))
    lower = 0.05
    root_lower = math.sqrt(lower)
    root_upper = 1.0 + 3.0 * cbar
    upper = root_upper * root_upper
    spread = upper - lower
    ratio = (root_upper - root_lower) / (root_upper + root_lower)
    keep = 2.0 * (2.0 - (upper + lower)) / spread
    once = -8.0 * cos_ref[...] * cbar / spread
    twice = 4.0 * cbar * cbar / spread
    weight = 2.0 / (root_upper * root_lower)
    for degree in range(ORDER + 1):
        weight_ref[degree : degree + 1, :] = weight
        weight = weight * -ratio
    half = side_x // 2

    def left(start, value):
        window = slice(start, start + half)
        return dot3((xh_ref[window], xl_ref[window]), value)

    def body(index, carry):
        ahead, second, _ = carry
        value = split(ahead)
        row = weight_ref[pl.ds(ORDER - 1 - index, 1), :]
        inner = [
            (split(left(start, value) * once), split(left(side_x + start, value) * twice)) for start in (0, half)
        ]
        parts = []
        for start, (single, double) in zip((0, half), inner):
            window = slice(start, start + half)
            hops = dot3(single, (yh_ref[:side_y], yl_ref[:side_y])) + dot3(double, (yh_ref[side_y:], yl_ref[side_y:]))
            parts.append((row * field[window] + keep * ahead[window] - second[window]) + hops)
        return jnp.concatenate(parts, axis=0), ahead, second

    ahead = weight_ref[ORDER : ORDER + 1, :] * field
    before = ahead - ahead
    result, _, second = lax.fori_loop(0, ORDER, body, (ahead, before, before), unroll=True)
    return 0.5 * (result - second)


def chebyshev_kernel(*refs):
    field_ref, sum_ref, cos_ref = refs[:3]
    out_ref, weight_ref = refs[-2:]
    mean_level = jnp.sum(sum_ref[...], axis=0, keepdims=True)
    total = chebyshev_sum(field_ref[...], mean_level, cos_ref, refs[3:7], weight_ref)
    out_ref[...] = total if len(refs) == 9 else total + refs[7][...]


def joined(weight_ref, base, part, refs, window):
    keep_ref, other_ref, last_ref, last_other_ref = refs
    side_y = last_ref.shape[1]
    columns = slice(part * side_y, (part + 1) * side_y)
    total = keep_ref[window, columns] + other_ref[window, columns]
    return total + (weight_ref[base + 2 * part] * last_ref[window] + weight_ref[base + 2 * part + 1] * last_other_ref[window])


def first_spectral_kernel(weight_ref, base, keep_ref, other_ref, last_ref, last_other_ref, cos_ref, *refs):
    hop_refs, (out_ref, mean_ref, row_ref) = refs[:4], refs[4:]
    side_x = out_ref.shape[0]
    sources = keep_ref, other_ref, last_ref, last_other_ref
    row = sum(ref[side_x : side_x + 1, :] for ref in sources)
    mean_level = jnp.broadcast_to(jnp.sum(row, axis=1, keepdims=True), row.shape)
    mean_ref[...] = mean_level
    field = joined(weight_ref, base, 0, sources, slice(0, side_x))
    out_ref[...] = chebyshev_sum(field, mean_level, cos_ref, hop_refs, row_ref)


def next_spectral_kernel(weight_ref, base, keep_ref, other_ref, last_ref, last_other_ref, cos_ref, *refs):
    hop_refs, (mean_ref, add_ref, out_ref, row_ref) = refs[:4], refs[4:]
    field = joined(weight_ref, base, 0, (keep_ref, other_ref, last_ref, last_other_ref), slice(None))
    out_ref[...] = chebyshev_sum(field, mean_ref[...], cos_ref, hop_refs, row_ref) + add_ref[...]


def pack_kernel(noise_ref, level_ref, packed_ref, damp_ref, held_ref, noise_sem, level_sem, *, scale):
    side_x = noise_ref.shape[0]
    noise_copy = pltpu.make_async_copy(noise_ref, packed_ref.at[pl.ds(0, side_x)], noise_sem)
    level_copy = pltpu.make_async_copy(level_ref, held_ref, level_sem)
    noise_copy.start()
    level_copy.start()
    level_copy.wait()
    levels = held_ref[...].astype(F32)
    damp_ref[...] = jnp.exp(-0.05 * (levels - MIDDLE))
    share = jnp.sum(levels, axis=0, keepdims=True) * scale
    packed_ref[side_x:] = jnp.broadcast_to(share, (packed_ref.shape[0] - side_x, share.shape[1]))
    noise_copy.wait()


def residual_parts(before, here, after, damp, damp_next, noise_ref, x_refs, y_refs, out_ref):
    side_x, side_y = here.shape
    half = side_x // 2
    windows = (slice(0, half), slice(half, side_x))
    y_pair = tuple(ref[:side_y] for ref in y_refs)

    def propagate(value):
        value = split(value)
        inner = [split(dot3((x_refs[0][window], x_refs[1][window]), value)) for window in windows]
        return [dot3(part, y_pair) for part in inner]

    moved = propagate(damp_next * here)
    forward_next = jnp.concatenate([after[window] - part for window, part in zip(windows, moved)], axis=0)
    moved = propagate(damp * before)
    carried = propagate(forward_next)
    for window, part, back in zip(windows, moved, carried):
        forward = here[window] - part
        out_ref[window] = noise_ref[window] - (forward - damp_next[window] * back)


def normal_kernel(
    even_ref, slices_ref, other_ref, damp_ref, damp_next_ref, noise_ref, xh_ref, xl_ref, yh_ref, yl_ref, out_ref
):
    side_y = other_ref.shape[1]
    even = even_ref[...] > 0.5
    far = slices_ref[:, :side_y]
    here = slices_ref[:, side_y:]
    near = other_ref[...]
    before = jnp.where(even, far, near)
    after = jnp.where(even, near, far)
    damps = damp_ref[...], damp_next_ref[...]
    residual_parts(before, here, after, *damps, noise_ref, (xh_ref, xl_ref), (yh_ref, yl_ref), out_ref)


def gather_kernel(*refs, outs, side_x, base):
    weight_ref, keep_ref, send_ref = refs[0], refs[-2], refs[-1]
    field_refs = refs[1:-2]
    rows_in, side_y = field_refs[0].shape
    count = len(field_refs)
    rows = 16

    def body(index, carry):
        window = pl.ds(pl.multiple_of(index * rows, rows), rows)
        fields = [ref[window, :] for ref in field_refs]
        for target, start, begin in ((keep_ref, 0, base), (send_ref, 2, base + outs * count)):
            for part in range(outs):
                place = begin + part * (count - start) - start
                total = weight_ref[place + start] * fields[start]
                for index_in in range(start + 1, count):
                    total = total + weight_ref[place + index_in] * fields[index_in]
                target[window, part * side_y : (part + 1) * side_y] = total
        return carry

    lax.fori_loop(0, side_x // rows, body, 0, unroll=4)
    if rows_in > side_x:
        extra = [ref[side_x:, :] for ref in field_refs]
        keep_ref[side_x:, :] = sum(extra)
        send_ref[side_x:, :] = sum(extra[2:])


def finish_kernel(weight_ref, base, keep_ref, other_ref, last_ref, last_other_ref, *refs):
    damp_ref, damp_next_ref, noise_ref, xh_ref, xl_ref, yh_ref, yl_ref = refs[:7]
    out_refs = refs[7:]
    sources = keep_ref, other_ref, last_ref, last_other_ref
    slices = [joined(weight_ref, base, part, sources, slice(None)) for part in range(3)]
    if len(out_refs) == 2:
        out_refs[1][...] = slices[1]
    damps = damp_ref[...], damp_next_ref[...]
    residual_parts(*slices, *damps, noise_ref, (xh_ref, xl_ref), (yh_ref, yl_ref), out_refs[0])


def basis_of(length):
    times = np.arange(length)
    phase = (2 * (times // 2)[:, None] + 1) * times[None, :] % (2 * length)
    angles = phase * (math.pi / length)
    basis = np.where((times % 2 == 0)[:, None], np.cos(angles), np.sin(angles))
    return basis, basis.T * (2.0 / length)


def times_of(inverse, slices):
    length = inverse.shape[0]
    outside = (slices < 0) | (slices >= length)
    return inverse[slices % length] * np.where(outside, -1.0, 1.0)[:, None]


def table_parts(matrix, rows):
    matrix = np.kron(matrix, np.eye(rows))
    high = matrix.astype(BF16)
    return jnp.asarray(high), jnp.asarray((matrix - high.astype(np.float64)).astype(BF16))


def ring_of(length):
    chips = length // 2
    return [*range(0, chips, 2), *reversed(range(1, chips, 2))]


def ring_pairs(length):
    path = ring_of(length)
    chips = len(path)
    pairs = []
    for place, chip in enumerate(path):
        pairs += [(2 * chip, 2 * path[place - 1]), (2 * chip + 1, 2 * path[(place + 1) % chips] + 1)]
    return pairs


def ring_weights(length, rows_of):
    path = ring_of(length)
    chips = len(path)
    reach = chips // 2
    gathers, finishes = [], []
    for device in range(length):
        core = device % 2
        place = path.index(device // 2)
        way = 2 * core - 1
        own, partner = rows_of(device), rows_of(device ^ 1)
        arrivals = [
            2 * path[(place - way * hop) % chips] + side for hop in range(reach) for side in (core, 1 - core)
        ]
        far = 2 * path[(place + reach) % chips]
        gathers.append(np.concatenate([own[:, arrivals].ravel(), partner[:, arrivals[2:]].ravel()]))
        finishes.append(own[:, [far + core, far + 1 - core]].ravel())
    return np.stack(gathers).astype(np.float32), np.stack(finishes).astype(np.float32)


def add_partners(value, axis, step):
    count = lax.axis_size(axis)
    value = jnp.sum(value, axis=0, keepdims=True)
    shifts = range(1, min(4, count // step))
    others = [lax.ppermute(value, axis, [(i, i ^ (step * shift)) for i in range(count)]) for shift in shifts]
    return jnp.concatenate([value] + others, axis=0)


def exchange(value, axis):
    count = lax.axis_size(axis)
    rows, columns = value.shape
    blocks = value.reshape(count, rows // count, columns)
    return lax.all_to_all(blocks, axis, split_axis=0, concat_axis=0, tiled=True).reshape(rows, columns)


def by_exchange(noise, phonon_level, hops, cosine):
    side_x, side_y = noise.shape
    length = lax.axis_size("tm")
    position = lax.axis_index("tm")
    rows = side_x // length
    field_shape = shape(side_x, side_y)
    levels = phonon_level.astype(F32)
    damp = jnp.exp(-0.05 * (levels - MIDDLE))
    mean_rows = jnp.full((1, side_y), jnp.sum(levels) / (length * side_x * side_y), F32)
    basis, inverse = basis_of(length)
    forward = table_parts(basis, rows)
    times = np.arange(length)
    far = times_of(inverse, np.where(times % 2 == 0, times - 1, times + 1))
    back = [jnp.concatenate(pair, axis=0) for pair in zip(table_parts(far, rows), table_parts(inverse, rows))]

    def chebyshev(field, *operands):
        scratch = [pltpu.VMEM((16, side_y), F32)]
        return call(chebyshev_kernel, field_shape, 7 + len(operands), scratch)(field, mean_rows, cosine, *hops, *operands)

    def spectrum(field, beside):
        block = call(transform_kernel, field_shape, 3)(exchange(field, "tm"), *forward)
        block, beside = lax.optimization_barrier((block, beside))
        return exchange(block, "tm"), beside

    def residual_of(components):
        block = exchange(components, "tm")
        slices = exchange(call(transform_kernel, shape(side_x, 2 * side_y), 3)(block, *back), "tm")
        here = slices[:, side_y:]
        other = lax.ppermute(here, "tm", [(i, i ^ 1) for i in range(length)])
        even = jnp.full((1, side_y), (position % 2 == 0).astype(F32), F32)
        return here, call(normal_kernel, field_shape, 10)(even, slices, other, damp, damp_next, noise, *hops)

    power_of_two = length & (length - 1) == 0
    mean_rows = add_partners(mean_rows, "tm", 1) if power_of_two else lax.psum(mean_rows, "tm")
    field, mean_rows = spectrum(noise, mean_rows)
    step = 4
    while power_of_two and step < length:
        mean_rows = add_partners(mean_rows, "tm", step)
        step *= 4
    damp_next = lax.ppermute(damp, "tm", [(i, (i - 1) % length) for i in range(length)])
    first = chebyshev(field)
    _, second_residual = residual_of(first)
    field, _ = spectrum(second_residual, cosine)
    return residual_of(chebyshev(field, first))


def by_ring(noise, phonon_level, hops, cosine):
    side_x, side_y = noise.shape
    length = lax.axis_size("tm")
    position = lax.axis_index("tm")
    reach = length // 4
    extra = 8
    field_shape = shape(side_x, side_y)
    basis, inverse = basis_of(length)
    hop = ring_pairs(length)
    swap = [(i, i ^ 1) for i in range(length)]

    tables = [
        *ring_weights(length, lambda device: basis[device : device + 1]),
        *ring_weights(length, lambda device: times_of(inverse, np.arange(device - 1, device + 2))),
    ]
    starts = np.cumsum([0] + [table.shape[1] for table in tables]).tolist()
    forward, back = starts[:2], starts[2:4]
    table = jnp.asarray(np.concatenate(tables, axis=1))
    weights = lax.dynamic_index_in_dim(table, position, 0, keepdims=False)

    def around(own, base, outs, beside):
        partner = lax.ppermute(own, "tm", swap)
        fields = [own, partner]
        for step in range(1, reach):
            own = lax.ppermute(own, "tm", hop)
            partner = lax.ppermute(partner, "tm", hop)
            fields += [own, partner]
            if step == 1:
                own, beside = lax.optimization_barrier((own, beside))
        last = lax.ppermute(own, "tm", hop)

        def kernel(*refs):
            gather_kernel(*refs, outs=outs, side_x=side_x, base=base[0])

        wide = shape(own.shape[0], outs * side_y)
        adds = 4 * outs * len(fields) * side_x * side_y
        keep, send = call(kernel, (wide, wide), len(fields), passes=adds, scalars=1)(beside[0], *fields)
        other = lax.ppermute(send, "tm", swap)
        last_other = lax.ppermute(last, "tm", swap)
        return (beside[0], keep, other, last, last_other), beside

    def based(kernel, base):
        def run(weight_ref, *refs):
            kernel(weight_ref, base[1], *refs)

        return run

    scratch = [pltpu.VMEM((16, side_y), F32)]
    work = 12 * ORDER * 2 * side_x * side_y * max(side_x, side_y)

    def pack(*refs):
        pack_kernel(*refs, scale=1.0 / (length * side_x * side_y))

    packed, damp = pl.pallas_call(
        pack,
        out_shape=(shape(side_x + extra, side_y), field_shape),
        in_specs=[pl.BlockSpec(memory_space=pltpu.HBM)] * 2,
        out_specs=(VMEM, VMEM),
        scratch_shapes=[pltpu.VMEM((side_x, side_y), jnp.int32), pltpu.SemaphoreType.DMA, pltpu.SemaphoreType.DMA],
        compiler_params=pltpu.CompilerParams(vmem_limit_bytes=16 << 20),
    )(*(pltpu.with_memory_space_constraint(array, pltpu.HBM) for array in (noise, phonon_level)))
    parts, (weights, hops) = around(packed, forward, 1, (weights, hops))
    damp_wrap = lax.ppermute(damp, "tm", [(0, length - 1)])
    damp_next = lax.ppermute(damp, "tm", [(i, i - 1) for i in range(1, length)])
    first_kernel, next_kernel = based(first_spectral_kernel, forward), based(next_spectral_kernel, forward)
    finish = based(finish_kernel, back)
    first_outs = (field_shape, shape(1, side_y))
    first, mean_level = call(first_kernel, first_outs, 9, scratch, work, 1)(*parts, cosine, *hops)
    first, damp_next, damp_wrap = lax.optimization_barrier((first, damp_next, damp_wrap))
    damp_next = damp_next + damp_wrap
    beside = (weights,)
    parts, beside = around(first, back, 3, beside)
    (second_residual,) = call(finish, (field_shape,), 11, scalars=1)(*parts, damp, damp_next, noise, *hops)
    parts, beside = around(second_residual, forward, 1, beside)
    total = call(next_kernel, field_shape, 11, scratch, work, 1)(*parts, cosine, *hops, mean_level, first)
    parts, beside = around(total, back, 3, beside)
    residual, result = call(finish, (field_shape,) * 2, 11, scalars=1)(*parts, damp, damp_next, noise, *hops)
    return result, residual


def per_device(noise, phonon_level, hop_x, hop_y):
    _, side_x, side_y = noise.shape
    length = lax.axis_size("tm")
    position = lax.axis_index("tm")
    cosine = jnp.cos((2 * (position // 2) + 1).astype(F32) * (math.pi / length))
    cosine = jnp.full((1, side_y), cosine, F32)
    hop_parts = (shape(2 * side_x, side_x, BF16),) * 2 + (shape(2 * side_y, side_y, BF16),) * 2
    hops = call(prepare_kernel, hop_parts, 2)(hop_x, hop_y)
    ring = length % 4 == 0 and 8 <= length <= 16 and side_x % 64 == 0
    result, residual = (by_ring if ring else by_exchange)(noise[0], phonon_level[0], hops, cosine)
    return result[None], residual[None]


def solution(mesh):
    return jax.shard_map(
        per_device,
        mesh=mesh,
        in_specs=(P(("grp", "tm"), None, None), P(("grp", "tm"), None, None), P(), P()),
        out_specs=(P(("grp", "tm"), None, None), P(("grp", "tm"), None, None)),
        check_vma=False,
    )
```

```python
import math

import jax
import jax.numpy as jnp
import numpy as np
from jax import lax
from jax.experimental import pallas as pl
from jax.experimental.pallas import tpu as pltpu
from jax.sharding import PartitionSpec as P


ORDER = 10
LEVELS = 17
MIDDLE = (LEVELS - 1) // 2
BF16 = jnp.bfloat16
F32 = jnp.float32
VMEM = pl.BlockSpec(memory_space=pltpu.VMEM)


def call(kernel, out_shape, count, scratch=(), passes=0, scalars=0):
    return pl.pallas_call(
        kernel,
        out_shape=out_shape,
        in_specs=[pl.BlockSpec(memory_space=pltpu.SMEM)] * scalars + [VMEM] * count,
        out_specs=jax.tree.map(lambda _: VMEM, out_shape),
        scratch_shapes=list(scratch),
        compiler_params=pltpu.CompilerParams(vmem_limit_bytes=16 << 20),
        cost_estimate=pl.CostEstimate(flops=passes, transcendentals=0, bytes_accessed=0) if passes else None,
    )


def shape(rows, columns, kind=F32):
    return jax.ShapeDtypeStruct((rows, columns), kind)


def split(value):
    high = value.astype(BF16)
    return high, (value - high.astype(F32)).astype(BF16)


def dot3(left, right):
    def dot(a, b):
        return jnp.dot(a, b, preferred_element_type=F32)

    return dot(left[0], right[0]) + (dot(left[1], right[0]) + dot(left[0], right[1]))


def prepare_kernel(hop_x_ref, hop_y_ref, xh_ref, xl_ref, yh_ref, yl_ref):
    for ref, high_ref, low_ref in ((hop_x_ref, xh_ref, xl_ref), (hop_y_ref, yh_ref, yl_ref)):
        side = ref.shape[0]
        hop = ref[...]
        square = jnp.dot(hop, hop, precision=lax.Precision.HIGHEST, preferred_element_type=F32)
        high_ref[:side], low_ref[:side] = split(hop)
        high_ref[side:], low_ref[side:] = split(square)


def transform_kernel(block_ref, th_ref, tl_ref, out_ref):
    rows, columns = block_ref.shape
    block = split(block_ref[...])
    result = dot3((th_ref[...], tl_ref[...]), block)
    for part in range(th_ref.shape[0] // rows):
        out_ref[:, part * columns : (part + 1) * columns] = result[part * rows : (part + 1) * rows]


def chebyshev_sum(field, mean_level, cos_ref, hop_refs, weight_ref):
    xh_ref, xl_ref, yh_ref, yl_ref = hop_refs
    side_x, side_y = field.shape
    cbar = jnp.exp(-0.05 * (mean_level - MIDDLE))
    lower = 0.05
    root_lower = math.sqrt(lower)
    root_upper = 1.0 + 3.0 * cbar
    upper = root_upper * root_upper
    spread = upper - lower
    ratio = (root_upper - root_lower) / (root_upper + root_lower)
    keep = 2.0 * (2.0 - (upper + lower)) / spread
    once = -8.0 * cos_ref[...] * cbar / spread
    twice = 4.0 * cbar * cbar / spread
    weight = 2.0 / (root_upper * root_lower)
    for degree in range(ORDER + 1):
        weight_ref[degree : degree + 1, :] = weight
        weight = weight * -ratio
    half = side_x // 2

    def left(start, value):
        window = slice(start, start + half)
        return dot3((xh_ref[window], xl_ref[window]), value)

    def body(index, carry):
        ahead, second, _ = carry
        value = split(ahead)
        row = weight_ref[pl.ds(ORDER - 1 - index, 1), :]
        inner = [
            (split(left(start, value) * once), split(left(side_x + start, value) * twice)) for start in (0, half)
        ]
        parts = []
        for start, (single, double) in zip((0, half), inner):
            window = slice(start, start + half)
            hops = dot3(single, (yh_ref[:side_y], yl_ref[:side_y])) + dot3(double, (yh_ref[side_y:], yl_ref[side_y:]))
            parts.append((row * field[window] + keep * ahead[window] - second[window]) + hops)
        return jnp.concatenate(parts, axis=0), ahead, second

    ahead = weight_ref[ORDER : ORDER + 1, :] * field
    before = ahead - ahead
    result, _, second = lax.fori_loop(0, ORDER, body, (ahead, before, before), unroll=True)
    return 0.5 * (result - second)


def chebyshev_kernel(*refs):
    field_ref, sum_ref, cos_ref = refs[:3]
    out_ref, weight_ref = refs[-2:]
    mean_level = jnp.sum(sum_ref[...], axis=0, keepdims=True)
    total = chebyshev_sum(field_ref[...], mean_level, cos_ref, refs[3:7], weight_ref)
    out_ref[...] = total if len(refs) == 9 else total + refs[7][...]


def joined(weight_ref, base, part, refs, window):
    keep_ref, other_ref, last, last_other = refs
    side_y = last.shape[1]
    columns = slice(part * side_y, (part + 1) * side_y)
    total = keep_ref[window, columns] + other_ref[window, columns]
    return total + (weight_ref[base + 2 * part] * last[window] + weight_ref[base + 2 * part + 1] * last_other[window])


def whole(refs):
    return jnp.concatenate([ref[...] for ref in refs[:2]]), jnp.concatenate([ref[...] for ref in refs[2:]])


def first_spectral_kernel(weight_ref, base, keep_ref, other_ref, last_ref, last_other_ref, cos_ref, *refs):
    hop_refs, (out_ref, mean_ref, row_ref) = refs[:4], refs[4:]
    side_x = out_ref.shape[0]
    sources = keep_ref, other_ref, last_ref, last_other_ref
    row = sum(ref[side_x : side_x + 1, :] for ref in sources)
    mean_level = jnp.broadcast_to(jnp.sum(row, axis=1, keepdims=True), row.shape)
    mean_ref[...] = mean_level
    field = joined(weight_ref, base, 0, sources, slice(0, side_x))
    out_ref[...] = chebyshev_sum(field, mean_level, cos_ref, hop_refs, row_ref)


def next_spectral_kernel(weight_ref, base, keep_ref, other_ref, *refs):
    cos_ref, hop_refs, (mean_ref, add_ref, out_ref, row_ref) = refs[4], refs[5:9], refs[9:]
    field = joined(weight_ref, base, 0, (keep_ref, other_ref, *whole(refs[:4])), slice(None))
    out_ref[...] = chebyshev_sum(field, mean_ref[...], cos_ref, hop_refs, row_ref) + add_ref[...]


def pack_kernel(noise_ref, level_ref, packed_ref, damp_ref, held_ref, noise_sem, level_sem, *, scale):
    side_x = noise_ref.shape[0]
    noise_copy = pltpu.make_async_copy(noise_ref, packed_ref.at[pl.ds(0, side_x)], noise_sem)
    level_copy = pltpu.make_async_copy(level_ref, held_ref, level_sem)
    noise_copy.start()
    level_copy.start()
    level_copy.wait()
    levels = held_ref[...].astype(F32)
    damp_ref[...] = jnp.exp(-0.05 * (levels - MIDDLE))
    share = jnp.sum(levels, axis=0, keepdims=True) * scale
    packed_ref[side_x:] = jnp.broadcast_to(share, (packed_ref.shape[0] - side_x, share.shape[1]))
    noise_copy.wait()


def residual_parts(before, here, after, damp, damp_next, noise_ref, x_refs, y_refs, out_ref):
    side_x, side_y = here.shape
    half = side_x // 2
    windows = (slice(0, half), slice(half, side_x))
    y_pair = tuple(ref[:side_y] for ref in y_refs)

    def propagate(value):
        value = split(value)
        inner = [split(dot3((x_refs[0][window], x_refs[1][window]), value)) for window in windows]
        return [dot3(part, y_pair) for part in inner]

    moved = propagate(damp_next * here)
    forward_next = jnp.concatenate([after[window] - part for window, part in zip(windows, moved)], axis=0)
    moved = propagate(damp * before)
    carried = propagate(forward_next)
    for window, part, back in zip(windows, moved, carried):
        forward = here[window] - part
        out_ref[window] = noise_ref[window] - (forward - damp_next[window] * back)


def normal_kernel(
    even_ref, slices_ref, other_ref, damp_ref, damp_next_ref, noise_ref, xh_ref, xl_ref, yh_ref, yl_ref, out_ref
):
    side_y = other_ref.shape[1]
    even = even_ref[...] > 0.5
    far = slices_ref[:, :side_y]
    here = slices_ref[:, side_y:]
    near = other_ref[...]
    before = jnp.where(even, far, near)
    after = jnp.where(even, near, far)
    damps = damp_ref[...], damp_next_ref[...]
    residual_parts(before, here, after, *damps, noise_ref, (xh_ref, xl_ref), (yh_ref, yl_ref), out_ref)


def gather_kernel(*refs, outs, side_x, base):
    weight_ref, keep_ref, send_ref = refs[0], refs[-2], refs[-1]
    field_refs = refs[1:-2]
    rows_in, side_y = field_refs[0].shape
    count = len(field_refs)
    rows = 16

    def body(index, carry):
        window = pl.ds(pl.multiple_of(index * rows, rows), rows)
        fields = [ref[window, :] for ref in field_refs]
        for target, start, begin in ((keep_ref, 0, base), (send_ref, 2, base + outs * count)):
            for part in range(outs):
                place = begin + part * (count - start) - start
                total = weight_ref[place + start] * fields[start]
                for index_in in range(start + 1, count):
                    total = total + weight_ref[place + index_in] * fields[index_in]
                target[window, part * side_y : (part + 1) * side_y] = total
        return carry

    lax.fori_loop(0, side_x // rows, body, 0, unroll=4)
    if rows_in > side_x:
        extra = [ref[side_x:, :] for ref in field_refs]
        keep_ref[side_x:, :] = sum(extra)
        send_ref[side_x:, :] = sum(extra[2:])


def gather_chunks_kernel(*refs, outs, base):
    weight_ref, keep_ref, send_ref = refs[0], refs[-2], refs[-1]
    own_ref, partner_ref = refs[1:3]
    hops = [refs[place : place + 3] for place in range(3, len(refs) - 2, 3)]
    side_x, side_y = own_ref.shape
    head = hops[0][0].shape[0]
    rest = side_x - head
    count = 2 + 2 * len(hops)
    rows = 16

    def body(index, carry):
        start = pl.multiple_of(index * rows, rows)
        window = pl.ds(start, rows)
        fields = [own_ref[window, :], partner_ref[window, :]]
        for first, middle, second in hops:
            fields.append(first[window, :] if carry[0] else middle[pl.ds(start - head, rows), :])
            fields.append(middle[pl.ds(start + rest, rows), :] if carry[1] else second[pl.ds(start - rest, rows), :])
        for target, skip, begin in ((keep_ref, 0, base), (send_ref, 2, base + outs * count)):
            for part in range(outs):
                place = begin + part * (count - skip) - skip
                total = weight_ref[place + skip] * fields[skip]
                for index_in in range(skip + 1, count):
                    total = total + weight_ref[place + index_in] * fields[index_in]
                target[window, part * side_y : (part + 1) * side_y] = total

    def run(low, high, in_first, in_middle):
        def step(index, carry):
            body(index, (in_first, in_middle))
            return carry

        lax.fori_loop(low // rows, high // rows, step, 0)

    run(0, rest, True, True)
    run(rest, head, True, False)
    run(head, side_x, False, False)


def finish_kernel(weight_ref, base, keep_ref, other_ref, *refs):
    damp_ref, damp_next_ref, noise_ref, xh_ref, xl_ref, yh_ref, yl_ref = refs[4:11]
    out_refs = refs[11:]
    sources = keep_ref, other_ref, *whole(refs[:4])
    slices = [joined(weight_ref, base, part, sources, slice(None)) for part in range(3)]
    if len(out_refs) == 2:
        out_refs[1][...] = slices[1]
    damps = damp_ref[...], damp_next_ref[...]
    residual_parts(*slices, *damps, noise_ref, (xh_ref, xl_ref), (yh_ref, yl_ref), out_refs[0])


def basis_of(length):
    times = np.arange(length)
    phase = (2 * (times // 2)[:, None] + 1) * times[None, :] % (2 * length)
    angles = phase * (math.pi / length)
    basis = np.where((times % 2 == 0)[:, None], np.cos(angles), np.sin(angles))
    return basis, basis.T * (2.0 / length)


def times_of(inverse, slices):
    length = inverse.shape[0]
    outside = (slices < 0) | (slices >= length)
    return inverse[slices % length] * np.where(outside, -1.0, 1.0)[:, None]


def table_parts(matrix, rows):
    matrix = np.kron(matrix, np.eye(rows))
    high = matrix.astype(BF16)
    return jnp.asarray(high), jnp.asarray((matrix - high.astype(np.float64)).astype(BF16))


def ring_of(length):
    chips = length // 2
    return [*range(0, chips, 2), *reversed(range(1, chips, 2))]


def ring_pairs(length):
    path = ring_of(length)
    chips = len(path)
    pairs = []
    for place, chip in enumerate(path):
        pairs += [(2 * chip, 2 * path[place - 1]), (2 * chip + 1, 2 * path[(place + 1) % chips] + 1)]
    return pairs


def ring_weights(length, rows_of):
    path = ring_of(length)
    chips = len(path)
    reach = chips // 2
    gathers, finishes = [], []
    for device in range(length):
        core = device % 2
        place = path.index(device // 2)
        way = 2 * core - 1
        own, partner = rows_of(device), rows_of(device ^ 1)
        arrivals = [
            2 * path[(place - way * hop) % chips] + side for hop in range(reach) for side in (core, 1 - core)
        ]
        far = 2 * path[(place + reach) % chips]
        gathers.append(np.concatenate([own[:, arrivals].ravel(), partner[:, arrivals[2:]].ravel()]))
        finishes.append(own[:, [far + core, far + 1 - core]].ravel())
    return np.stack(gathers).astype(np.float32), np.stack(finishes).astype(np.float32)


def add_partners(value, axis, step):
    count = lax.axis_size(axis)
    value = jnp.sum(value, axis=0, keepdims=True)
    shifts = range(1, min(4, count // step))
    others = [lax.ppermute(value, axis, [(i, i ^ (step * shift)) for i in range(count)]) for shift in shifts]
    return jnp.concatenate([value] + others, axis=0)


def exchange(value, axis):
    count = lax.axis_size(axis)
    rows, columns = value.shape
    blocks = value.reshape(count, rows // count, columns)
    return lax.all_to_all(blocks, axis, split_axis=0, concat_axis=0, tiled=True).reshape(rows, columns)


def by_exchange(noise, phonon_level, hops, cosine):
    side_x, side_y = noise.shape
    length = lax.axis_size("tm")
    position = lax.axis_index("tm")
    rows = side_x // length
    field_shape = shape(side_x, side_y)
    levels = phonon_level.astype(F32)
    damp = jnp.exp(-0.05 * (levels - MIDDLE))
    mean_rows = jnp.full((1, side_y), jnp.sum(levels) / (length * side_x * side_y), F32)
    basis, inverse = basis_of(length)
    forward = table_parts(basis, rows)
    times = np.arange(length)
    far = times_of(inverse, np.where(times % 2 == 0, times - 1, times + 1))
    back = [jnp.concatenate(pair, axis=0) for pair in zip(table_parts(far, rows), table_parts(inverse, rows))]

    def chebyshev(field, *operands):
        scratch = [pltpu.VMEM((16, side_y), F32)]
        return call(chebyshev_kernel, field_shape, 7 + len(operands), scratch)(field, mean_rows, cosine, *hops, *operands)

    def spectrum(field, beside):
        block = call(transform_kernel, field_shape, 3)(exchange(field, "tm"), *forward)
        block, beside = lax.optimization_barrier((block, beside))
        return exchange(block, "tm"), beside

    def residual_of(components):
        block = exchange(components, "tm")
        slices = exchange(call(transform_kernel, shape(side_x, 2 * side_y), 3)(block, *back), "tm")
        here = slices[:, side_y:]
        other = lax.ppermute(here, "tm", [(i, i ^ 1) for i in range(length)])
        even = jnp.full((1, side_y), (position % 2 == 0).astype(F32), F32)
        return here, call(normal_kernel, field_shape, 10)(even, slices, other, damp, damp_next, noise, *hops)

    power_of_two = length & (length - 1) == 0
    mean_rows = add_partners(mean_rows, "tm", 1) if power_of_two else lax.psum(mean_rows, "tm")
    field, mean_rows = spectrum(noise, mean_rows)
    step = 4
    while power_of_two and step < length:
        mean_rows = add_partners(mean_rows, "tm", step)
        step *= 4
    damp_next = lax.ppermute(damp, "tm", [(i, (i - 1) % length) for i in range(length)])
    first = chebyshev(field)
    _, second_residual = residual_of(first)
    field, _ = spectrum(second_residual, cosine)
    return residual_of(chebyshev(field, first))


def by_ring(noise, phonon_level, hops, cosine):
    side_x, side_y = noise.shape
    length = lax.axis_size("tm")
    position = lax.axis_index("tm")
    reach = length // 4
    extra = 8
    field_shape = shape(side_x, side_y)
    basis, inverse = basis_of(length)
    hop = ring_pairs(length)
    swap = [(i, i ^ 1) for i in range(length)]

    tables = [
        *ring_weights(length, lambda device: basis[device : device + 1]),
        *ring_weights(length, lambda device: times_of(inverse, np.arange(device - 1, device + 2))),
    ]
    starts = np.cumsum([0] + [table.shape[1] for table in tables]).tolist()
    forward, back = starts[:2], starts[2:4]
    table = jnp.asarray(np.concatenate(tables, axis=1))
    weights = lax.dynamic_index_in_dim(table, position, 0, keepdims=False)

    def around(own, base, outs, beside):
        partner = lax.ppermute(own, "tm", swap)
        fields = [own, partner]
        for step in range(1, reach):
            own = lax.ppermute(own, "tm", hop)
            partner = lax.ppermute(partner, "tm", hop)
            fields += [own, partner]
            if step == 1:
                own, beside = lax.optimization_barrier((own, beside))
        last = lax.ppermute(own, "tm", hop)

        def kernel(*refs):
            gather_kernel(*refs, outs=outs, side_x=side_x, base=base[0])

        wide = shape(own.shape[0], outs * side_y)
        adds = 4 * outs * len(fields) * side_x * side_y
        keep, send = call(kernel, (wide, wide), len(fields), passes=adds, scalars=1)(beside[0], *fields)
        other = lax.ppermute(send, "tm", swap)
        last_other = lax.ppermute(last, "tm", swap)
        return (beside[0], keep, other, last, last_other), beside

    def around_in_chunks(own, base, outs, weights):
        head = (side_x * 11 // 16) // 16 * 16
        rest = side_x - head
        partner = lax.ppermute(own, "tm", swap)
        chunks = [own[:head], jnp.concatenate([own[head:], partner[:rest]]), partner[rest:]]
        fields = [own, partner]
        for _ in range(1, reach):
            first = lax.ppermute(chunks[0], "tm", hop)
            chunks = [first] + [lax.ppermute(chunk, "tm", hop) for chunk in chunks[1:]]
            fields += chunks
        last = lax.ppermute(chunks[0], "tm", hop)
        tail = lax.ppermute(chunks[1][:rest], "tm", hop)

        def kernel(*refs):
            gather_chunks_kernel(*refs, outs=outs, base=base[0])

        wide = shape(side_x, outs * side_y)
        adds = 4 * outs * len(fields) * side_x * side_y
        keep, send = call(kernel, (wide, wide), len(fields), passes=adds, scalars=1)(weights, *fields)
        other = lax.ppermute(send, "tm", swap)
        last_other = lax.ppermute(last, "tm", swap)
        tail_other = lax.ppermute(tail, "tm", swap)
        return weights, keep, other, last, tail, last_other, tail_other

    def based(kernel, base):
        def run(weight_ref, *refs):
            kernel(weight_ref, base[1], *refs)

        return run

    scratch = [pltpu.VMEM((16, side_y), F32)]
    work = 12 * ORDER * 2 * side_x * side_y * max(side_x, side_y)

    def pack(*refs):
        pack_kernel(*refs, scale=1.0 / (length * side_x * side_y))

    packed, damp = pl.pallas_call(
        pack,
        out_shape=(shape(side_x + extra, side_y), field_shape),
        in_specs=[pl.BlockSpec(memory_space=pltpu.HBM)] * 2,
        out_specs=(VMEM, VMEM),
        scratch_shapes=[pltpu.VMEM((side_x, side_y), jnp.int32), pltpu.SemaphoreType.DMA, pltpu.SemaphoreType.DMA],
        compiler_params=pltpu.CompilerParams(vmem_limit_bytes=16 << 20),
    )(*(pltpu.with_memory_space_constraint(array, pltpu.HBM) for array in (noise, phonon_level)))
    parts, (weights, hops) = around(packed, forward, 1, (weights, hops))
    damp_wrap = lax.ppermute(damp, "tm", [(0, length - 1)])
    damp_next = lax.ppermute(damp, "tm", [(i, i - 1) for i in range(1, length)])
    first_kernel, next_kernel = based(first_spectral_kernel, forward), based(next_spectral_kernel, forward)
    finish = based(finish_kernel, back)
    first_outs = (field_shape, shape(1, side_y))
    first, mean_level = call(first_kernel, first_outs, 9, scratch, work, 1)(*parts, cosine, *hops)
    first, damp_next, damp_wrap = lax.optimization_barrier((first, damp_next, damp_wrap))
    damp_next = damp_next + damp_wrap
    parts = around_in_chunks(first, back, 3, weights)
    (second_residual,) = call(finish, (field_shape,), 13, scalars=1)(*parts, damp, damp_next, noise, *hops)
    parts = around_in_chunks(second_residual, forward, 1, weights)
    total = call(next_kernel, field_shape, 13, scratch, work, 1)(*parts, cosine, *hops, mean_level, first)
    parts = around_in_chunks(total, back, 3, weights)
    residual, result = call(finish, (field_shape,) * 2, 13, scalars=1)(*parts, damp, damp_next, noise, *hops)
    return result, residual


def per_device(noise, phonon_level, hop_x, hop_y):
    _, side_x, side_y = noise.shape
    length = lax.axis_size("tm")
    position = lax.axis_index("tm")
    cosine = jnp.cos((2 * (position // 2) + 1).astype(F32) * (math.pi / length))
    cosine = jnp.full((1, side_y), cosine, F32)
    hop_parts = (shape(2 * side_x, side_x, BF16),) * 2 + (shape(2 * side_y, side_y, BF16),) * 2
    hops = call(prepare_kernel, hop_parts, 2)(hop_x, hop_y)
    ring = length % 4 == 0 and 8 <= length <= 16 and side_x % 64 == 0
    result, residual = (by_ring if ring else by_exchange)(noise[0], phonon_level[0], hops, cosine)
    return result[None], residual[None]


def solution(mesh):
    return jax.shard_map(
        per_device,
        mesh=mesh,
        in_specs=(P(("grp", "tm"), None, None), P(("grp", "tm"), None, None), P(), P()),
        out_specs=(P(("grp", "tm"), None, None), P(("grp", "tm"), None, None)),
        check_vma=False,
    )
```

```python
import math

import jax
import jax.numpy as jnp
import numpy as np
from jax import lax
from jax.experimental import pallas as pl
from jax.experimental.pallas import tpu as pltpu
from jax.sharding import PartitionSpec as P


ORDER = 10
LEVELS = 17
MIDDLE = (LEVELS - 1) // 2
BF16 = jnp.bfloat16
F32 = jnp.float32
VMEM = pl.BlockSpec(memory_space=pltpu.VMEM)


def call(kernel, out_shape, count, scratch=(), passes=0, scalars=0):
    return pl.pallas_call(
        kernel,
        out_shape=out_shape,
        in_specs=[pl.BlockSpec(memory_space=pltpu.SMEM)] * scalars + [VMEM] * count,
        out_specs=jax.tree.map(lambda _: VMEM, out_shape),
        scratch_shapes=list(scratch),
        compiler_params=pltpu.CompilerParams(vmem_limit_bytes=16 << 20),
        cost_estimate=pl.CostEstimate(flops=passes, transcendentals=0, bytes_accessed=0) if passes else None,
    )


def shape(rows, columns, kind=F32):
    return jax.ShapeDtypeStruct((rows, columns), kind)


def split(value):
    high = value.astype(BF16)
    return high, (value - high.astype(F32)).astype(BF16)


def dot3(left, right):
    def dot(a, b):
        return jnp.dot(a, b, preferred_element_type=F32)

    return dot(left[0], right[0]) + (dot(left[1], right[0]) + dot(left[0], right[1]))


def prepare_kernel(hop_x_ref, hop_y_ref, xh_ref, xl_ref, yh_ref, yl_ref):
    for ref, high_ref, low_ref in ((hop_x_ref, xh_ref, xl_ref), (hop_y_ref, yh_ref, yl_ref)):
        side = ref.shape[0]
        hop = ref[...]
        square = jnp.dot(hop, hop, precision=lax.Precision.HIGHEST, preferred_element_type=F32)
        high_ref[:side], low_ref[:side] = split(hop)
        high_ref[side:], low_ref[side:] = split(square)


def transform_kernel(block_ref, th_ref, tl_ref, out_ref):
    rows, columns = block_ref.shape
    block = split(block_ref[...])
    result = dot3((th_ref[...], tl_ref[...]), block)
    for part in range(th_ref.shape[0] // rows):
        out_ref[:, part * columns : (part + 1) * columns] = result[part * rows : (part + 1) * rows]


def chebyshev_sum(field, mean_level, cos_ref, hop_refs, weight_ref):
    xh_ref, xl_ref, yh_ref, yl_ref = hop_refs
    side_x, side_y = field.shape
    cbar = jnp.exp(-0.05 * (mean_level - MIDDLE))
    lower = 0.05
    root_lower = math.sqrt(lower)
    root_upper = 1.0 + 3.0 * cbar
    upper = root_upper * root_upper
    spread = upper - lower
    ratio = (root_upper - root_lower) / (root_upper + root_lower)
    keep = 2.0 * (2.0 - (upper + lower)) / spread
    once = -8.0 * cos_ref[...] * cbar / spread
    twice = 4.0 * cbar * cbar / spread
    weight = 2.0 / (root_upper * root_lower)
    for degree in range(ORDER + 1):
        weight_ref[degree : degree + 1, :] = weight
        weight = weight * -ratio
    half = side_x // 2

    def left(start, value):
        window = slice(start, start + half)
        return dot3((xh_ref[window], xl_ref[window]), value)

    def body(index, carry):
        ahead, second, _ = carry
        value = split(ahead)
        row = weight_ref[pl.ds(ORDER - 1 - index, 1), :]
        inner = [
            (split(left(start, value) * once), split(left(side_x + start, value) * twice)) for start in (0, half)
        ]
        parts = []
        for start, (single, double) in zip((0, half), inner):
            window = slice(start, start + half)
            hops = dot3(single, (yh_ref[:side_y], yl_ref[:side_y])) + dot3(double, (yh_ref[side_y:], yl_ref[side_y:]))
            parts.append((row * field[window] + keep * ahead[window] - second[window]) + hops)
        return jnp.concatenate(parts, axis=0), ahead, second

    ahead = weight_ref[ORDER : ORDER + 1, :] * field
    before = ahead - ahead
    result, _, second = lax.fori_loop(0, ORDER, body, (ahead, before, before), unroll=True)
    return 0.5 * (result - second)


def chebyshev_kernel(*refs):
    field_ref, sum_ref, cos_ref = refs[:3]
    out_ref, weight_ref = refs[-2:]
    mean_level = jnp.sum(sum_ref[...], axis=0, keepdims=True)
    total = chebyshev_sum(field_ref[...], mean_level, cos_ref, refs[3:7], weight_ref)
    out_ref[...] = total if len(refs) == 9 else total + refs[7][...]


def joined(weight_ref, base, part, refs, window):
    keep_ref, other_ref, last, last_other = refs
    side_y = last.shape[1]
    columns = slice(part * side_y, (part + 1) * side_y)
    total = keep_ref[window, columns] + other_ref[window, columns]
    return total + (weight_ref[base + 2 * part] * last[window] + weight_ref[base + 2 * part + 1] * last_other[window])


def whole(refs):
    return jnp.concatenate([ref[...] for ref in refs[:2]]), jnp.concatenate([ref[...] for ref in refs[2:]])


def first_spectral_kernel(weight_ref, base, keep_ref, other_ref, last_ref, last_other_ref, cos_ref, *refs):
    hop_refs, (out_ref, mean_ref, row_ref) = refs[:4], refs[4:]
    side_x = out_ref.shape[0]
    sources = keep_ref, other_ref, last_ref, last_other_ref
    row = sum(ref[side_x : side_x + 1, :] for ref in sources)
    mean_level = jnp.broadcast_to(jnp.sum(row, axis=1, keepdims=True), row.shape)
    mean_ref[...] = mean_level
    field = joined(weight_ref, base, 0, sources, slice(0, side_x))
    out_ref[...] = chebyshev_sum(field, mean_level, cos_ref, hop_refs, row_ref)


def next_spectral_kernel(weight_ref, base, keep_ref, other_ref, *refs):
    cos_ref, hop_refs, (mean_ref, add_ref, out_ref, row_ref) = refs[4], refs[5:9], refs[9:]
    field = joined(weight_ref, base, 0, (keep_ref, other_ref, *whole(refs[:4])), slice(None))
    out_ref[...] = chebyshev_sum(field, mean_ref[...], cos_ref, hop_refs, row_ref) + add_ref[...]


def pack_kernel(noise_ref, level_ref, packed_ref, damp_ref, held_ref, noise_sem, level_sem, *, scale):
    side_x = noise_ref.shape[0]
    noise_copy = pltpu.make_async_copy(noise_ref, packed_ref.at[pl.ds(0, side_x)], noise_sem)
    level_copy = pltpu.make_async_copy(level_ref, held_ref, level_sem)
    noise_copy.start()
    level_copy.start()
    level_copy.wait()
    levels = held_ref[...].astype(F32)
    damp_ref[...] = jnp.exp(-0.05 * (levels - MIDDLE))
    share = jnp.sum(levels, axis=0, keepdims=True) * scale
    packed_ref[side_x:] = jnp.broadcast_to(share, (packed_ref.shape[0] - side_x, share.shape[1]))
    noise_copy.wait()


def residual_parts(before, here, after, damp, damp_next, noise_ref, x_refs, y_refs, out_ref):
    side_x, side_y = here.shape
    half = side_x // 2
    windows = (slice(0, half), slice(half, side_x))
    y_pair = tuple(ref[:side_y] for ref in y_refs)

    def propagate(value):
        value = split(value)
        inner = [split(dot3((x_refs[0][window], x_refs[1][window]), value)) for window in windows]
        return [dot3(part, y_pair) for part in inner]

    moved = propagate(damp_next * here)
    forward_next = jnp.concatenate([after[window] - part for window, part in zip(windows, moved)], axis=0)
    moved = propagate(damp * before)
    carried = propagate(forward_next)
    for window, part, back in zip(windows, moved, carried):
        forward = here[window] - part
        out_ref[window] = noise_ref[window] - (forward - damp_next[window] * back)


def normal_kernel(
    even_ref, slices_ref, other_ref, damp_ref, damp_next_ref, noise_ref, xh_ref, xl_ref, yh_ref, yl_ref, out_ref
):
    side_y = other_ref.shape[1]
    even = even_ref[...] > 0.5
    far = slices_ref[:, :side_y]
    here = slices_ref[:, side_y:]
    near = other_ref[...]
    before = jnp.where(even, far, near)
    after = jnp.where(even, near, far)
    damps = damp_ref[...], damp_next_ref[...]
    residual_parts(before, here, after, *damps, noise_ref, (xh_ref, xl_ref), (yh_ref, yl_ref), out_ref)


def gather_kernel(*refs, outs, side_x, base):
    weight_ref, keep_ref, send_ref = refs[0], refs[-2], refs[-1]
    field_refs = refs[1:-2]
    rows_in, side_y = field_refs[0].shape
    count = len(field_refs)
    rows = 16

    def body(index, carry):
        window = pl.ds(pl.multiple_of(index * rows, rows), rows)
        fields = [ref[window, :] for ref in field_refs]
        for target, start, begin in ((keep_ref, 0, base), (send_ref, 2, base + outs * count)):
            for part in range(outs):
                place = begin + part * (count - start) - start
                total = weight_ref[place + start] * fields[start]
                for index_in in range(start + 1, count):
                    total = total + weight_ref[place + index_in] * fields[index_in]
                target[window, part * side_y : (part + 1) * side_y] = total
        return carry

    lax.fori_loop(0, side_x // rows, body, 0, unroll=4)
    if rows_in > side_x:
        extra = [ref[side_x:, :] for ref in field_refs]
        keep_ref[side_x:, :] = sum(extra)
        send_ref[side_x:, :] = sum(extra[2:])


def gather_chunks_kernel(*refs, outs, base):
    weight_ref, keep_ref, send_ref = refs[0], refs[-2], refs[-1]
    own_ref, partner_ref = refs[1:3]
    hops = [refs[place : place + 3] for place in range(3, len(refs) - 2, 3)]
    side_x, side_y = own_ref.shape
    head = hops[0][0].shape[0]
    rest = side_x - head
    count = 2 + 2 * len(hops)
    rows = 16

    def body(index, carry):
        start = pl.multiple_of(index * rows, rows)
        window = pl.ds(start, rows)
        fields = [own_ref[window, :], partner_ref[window, :]]
        for first, middle, second in hops:
            fields.append(first[window, :] if carry[0] else middle[pl.ds(start - head, rows), :])
            fields.append(middle[pl.ds(start + rest, rows), :] if carry[1] else second[pl.ds(start - rest, rows), :])
        for target, skip, begin in ((keep_ref, 0, base), (send_ref, 2, base + outs * count)):
            for part in range(outs):
                place = begin + part * (count - skip) - skip
                total = weight_ref[place + skip] * fields[skip]
                for index_in in range(skip + 1, count):
                    total = total + weight_ref[place + index_in] * fields[index_in]
                target[window, part * side_y : (part + 1) * side_y] = total

    def run(low, high, in_first, in_middle):
        def step(index, carry):
            body(index, (in_first, in_middle))
            return carry

        lax.fori_loop(low // rows, high // rows, step, 0)

    run(0, rest, True, True)
    run(rest, head, True, False)
    run(head, side_x, False, False)


def finish_kernel(weight_ref, base, keep_ref, other_ref, *refs):
    damp_ref, damp_next_ref, noise_ref, xh_ref, xl_ref, yh_ref, yl_ref = refs[4:11]
    out_refs = refs[11:]
    sources = keep_ref, other_ref, *whole(refs[:4])
    slices = [joined(weight_ref, base, part, sources, slice(None)) for part in range(3)]
    if len(out_refs) == 2:
        out_refs[1][...] = slices[1]
    damps = damp_ref[...], damp_next_ref[...]
    residual_parts(*slices, *damps, noise_ref, (xh_ref, xl_ref), (yh_ref, yl_ref), out_refs[0])


def basis_of(length):
    times = np.arange(length)
    phase = (2 * (times // 2)[:, None] + 1) * times[None, :] % (2 * length)
    angles = phase * (math.pi / length)
    basis = np.where((times % 2 == 0)[:, None], np.cos(angles), np.sin(angles))
    return basis, basis.T * (2.0 / length)


def times_of(inverse, slices):
    length = inverse.shape[0]
    outside = (slices < 0) | (slices >= length)
    return inverse[slices % length] * np.where(outside, -1.0, 1.0)[:, None]


def table_parts(matrix, rows):
    matrix = np.kron(matrix, np.eye(rows))
    high = matrix.astype(BF16)
    return jnp.asarray(high), jnp.asarray((matrix - high.astype(np.float64)).astype(BF16))


def ring_of(length):
    chips = length // 2
    return [*range(0, chips, 2), *reversed(range(1, chips, 2))]


def ring_pairs(length):
    path = ring_of(length)
    chips = len(path)
    pairs = []
    for place, chip in enumerate(path):
        pairs += [(2 * chip, 2 * path[place - 1]), (2 * chip + 1, 2 * path[(place + 1) % chips] + 1)]
    return pairs


def ring_weights(length, rows_of):
    path = ring_of(length)
    chips = len(path)
    reach = chips // 2
    gathers, finishes = [], []
    for device in range(length):
        core = device % 2
        place = path.index(device // 2)
        way = 2 * core - 1
        own, partner = rows_of(device), rows_of(device ^ 1)
        arrivals = [
            2 * path[(place - way * hop) % chips] + side for hop in range(reach) for side in (core, 1 - core)
        ]
        far = 2 * path[(place + reach) % chips]
        gathers.append(np.concatenate([own[:, arrivals].ravel(), partner[:, arrivals[2:]].ravel()]))
        finishes.append(own[:, [far + core, far + 1 - core]].ravel())
    return np.stack(gathers).astype(np.float32), np.stack(finishes).astype(np.float32)


def add_partners(value, axis, step):
    count = lax.axis_size(axis)
    value = jnp.sum(value, axis=0, keepdims=True)
    shifts = range(1, min(4, count // step))
    others = [lax.ppermute(value, axis, [(i, i ^ (step * shift)) for i in range(count)]) for shift in shifts]
    return jnp.concatenate([value] + others, axis=0)


def exchange(value, axis):
    count = lax.axis_size(axis)
    rows, columns = value.shape
    blocks = value.reshape(count, rows // count, columns)
    return lax.all_to_all(blocks, axis, split_axis=0, concat_axis=0, tiled=True).reshape(rows, columns)


def by_exchange(noise, phonon_level, hops, cosine):
    side_x, side_y = noise.shape
    length = lax.axis_size("tm")
    position = lax.axis_index("tm")
    rows = side_x // length
    field_shape = shape(side_x, side_y)
    levels = phonon_level.astype(F32)
    damp = jnp.exp(-0.05 * (levels - MIDDLE))
    mean_rows = jnp.full((1, side_y), jnp.sum(levels) / (length * side_x * side_y), F32)
    basis, inverse = basis_of(length)
    forward = table_parts(basis, rows)
    times = np.arange(length)
    far = times_of(inverse, np.where(times % 2 == 0, times - 1, times + 1))
    back = [jnp.concatenate(pair, axis=0) for pair in zip(table_parts(far, rows), table_parts(inverse, rows))]

    def chebyshev(field, *operands):
        scratch = [pltpu.VMEM((16, side_y), F32)]
        return call(chebyshev_kernel, field_shape, 7 + len(operands), scratch)(field, mean_rows, cosine, *hops, *operands)

    def spectrum(field, beside):
        block = call(transform_kernel, field_shape, 3)(exchange(field, "tm"), *forward)
        block, beside = lax.optimization_barrier((block, beside))
        return exchange(block, "tm"), beside

    def residual_of(components):
        block = exchange(components, "tm")
        slices = exchange(call(transform_kernel, shape(side_x, 2 * side_y), 3)(block, *back), "tm")
        here = slices[:, side_y:]
        other = lax.ppermute(here, "tm", [(i, i ^ 1) for i in range(length)])
        even = jnp.full((1, side_y), (position % 2 == 0).astype(F32), F32)
        return here, call(normal_kernel, field_shape, 10)(even, slices, other, damp, damp_next, noise, *hops)

    power_of_two = length & (length - 1) == 0
    mean_rows = add_partners(mean_rows, "tm", 1) if power_of_two else lax.psum(mean_rows, "tm")
    field, mean_rows = spectrum(noise, mean_rows)
    step = 4
    while power_of_two and step < length:
        mean_rows = add_partners(mean_rows, "tm", step)
        step *= 4
    damp_next = lax.ppermute(damp, "tm", [(i, (i - 1) % length) for i in range(length)])
    first = chebyshev(field)
    _, second_residual = residual_of(first)
    field, _ = spectrum(second_residual, cosine)
    return residual_of(chebyshev(field, first))


def by_ring(noise, phonon_level, hops, cosine):
    side_x, side_y = noise.shape
    length = lax.axis_size("tm")
    position = lax.axis_index("tm")
    reach = length // 4
    extra = 8
    field_shape = shape(side_x, side_y)
    basis, inverse = basis_of(length)
    hop = ring_pairs(length)
    swap = [(i, i ^ 1) for i in range(length)]

    tables = [
        *ring_weights(length, lambda device: basis[device : device + 1]),
        *ring_weights(length, lambda device: times_of(inverse, np.arange(device - 1, device + 2))),
    ]
    starts = np.cumsum([0] + [table.shape[1] for table in tables]).tolist()
    forward, back = starts[:2], starts[2:4]
    table = jnp.asarray(np.concatenate(tables, axis=1))
    weights = lax.dynamic_index_in_dim(table, position, 0, keepdims=False)

    def around(own, base, outs, beside):
        partner = lax.ppermute(own, "tm", swap)
        fields = [own, partner]
        for step in range(1, reach):
            own = lax.ppermute(own, "tm", hop)
            partner = lax.ppermute(partner, "tm", hop)
            fields += [own, partner]
            if step == 1:
                own, beside = lax.optimization_barrier((own, beside))
        last = lax.ppermute(own, "tm", hop)

        def kernel(*refs):
            gather_kernel(*refs, outs=outs, side_x=side_x, base=base[0])

        wide = shape(own.shape[0], outs * side_y)
        adds = 4 * outs * len(fields) * side_x * side_y
        keep, send = call(kernel, (wide, wide), len(fields), passes=adds, scalars=1)(beside[0], *fields)
        other = lax.ppermute(send, "tm", swap)
        last_other = lax.ppermute(last, "tm", swap)
        return (beside[0], keep, other, last, last_other), beside

    def around_in_chunks(own, base, outs, weights):
        head = (side_x * 3 // 4) // 16 * 16
        rest = side_x - head
        partner = lax.ppermute(own, "tm", swap)
        chunks = [own[:head], jnp.concatenate([own[head:], partner[:rest]]), partner[rest:]]
        fields = [own, partner]
        for _ in range(1, reach):
            first = lax.ppermute(chunks[0], "tm", hop)
            middle = lax.ppermute(chunks[1], "tm", hop)
            second = lax.ppermute(chunks[2], "tm", hop)
            chunks = [first, middle, second]
            fields += chunks
        last = lax.ppermute(chunks[0], "tm", hop)
        tail = lax.ppermute(chunks[1][:rest], "tm", hop)

        def kernel(*refs):
            gather_chunks_kernel(*refs, outs=outs, base=base[0])

        wide = shape(side_x, outs * side_y)
        adds = 4 * outs * len(fields) * side_x * side_y
        keep, send = call(kernel, (wide, wide), len(fields), passes=adds, scalars=1)(weights, *fields)
        other = lax.ppermute(send, "tm", swap)
        last_other = lax.ppermute(last, "tm", swap)
        tail_other = lax.ppermute(tail, "tm", swap)
        return weights, keep, other, last, tail, last_other, tail_other

    def based(kernel, base):
        def run(weight_ref, *refs):
            kernel(weight_ref, base[1], *refs)

        return run

    scratch = [pltpu.VMEM((16, side_y), F32)]
    work = 12 * ORDER * 2 * side_x * side_y * max(side_x, side_y)

    def pack(*refs):
        pack_kernel(*refs, scale=1.0 / (length * side_x * side_y))

    packed, damp = pl.pallas_call(
        pack,
        out_shape=(shape(side_x + extra, side_y), field_shape),
        in_specs=[pl.BlockSpec(memory_space=pltpu.HBM)] * 2,
        out_specs=(VMEM, VMEM),
        scratch_shapes=[pltpu.VMEM((side_x, side_y), jnp.int32), pltpu.SemaphoreType.DMA, pltpu.SemaphoreType.DMA],
        compiler_params=pltpu.CompilerParams(vmem_limit_bytes=16 << 20),
    )(*(pltpu.with_memory_space_constraint(array, pltpu.HBM) for array in (noise, phonon_level)))
    parts, (weights, hops) = around(packed, forward, 1, (weights, hops))
    damp_wrap = lax.ppermute(damp, "tm", [(0, length - 1)])
    damp_next = lax.ppermute(damp, "tm", [(i, i - 1) for i in range(1, length)])
    first_kernel, next_kernel = based(first_spectral_kernel, forward), based(next_spectral_kernel, forward)
    finish = based(finish_kernel, back)
    first_outs = (field_shape, shape(1, side_y))
    first, mean_level = call(first_kernel, first_outs, 9, scratch, work, 1)(*parts, cosine, *hops)
    first, damp_next, damp_wrap = lax.optimization_barrier((first, damp_next, damp_wrap))
    damp_next = damp_next + damp_wrap
    parts = around_in_chunks(first, back, 3, weights)
    (second_residual,) = call(finish, (field_shape,), 13, scalars=1)(*parts, damp, damp_next, noise, *hops)
    parts = around_in_chunks(second_residual, forward, 1, weights)
    total = call(next_kernel, field_shape, 13, scratch, work, 1)(*parts, cosine, *hops, mean_level, first)
    parts = around_in_chunks(total, back, 3, weights)
    residual, result = call(finish, (field_shape,) * 2, 13, scalars=1)(*parts, damp, damp_next, noise, *hops)
    return result, residual


def per_device(noise, phonon_level, hop_x, hop_y):
    _, side_x, side_y = noise.shape
    length = lax.axis_size("tm")
    position = lax.axis_index("tm")
    cosine = jnp.cos((2 * (position // 2) + 1).astype(F32) * (math.pi / length))
    cosine = jnp.full((1, side_y), cosine, F32)
    hop_parts = (shape(2 * side_x, side_x, BF16),) * 2 + (shape(2 * side_y, side_y, BF16),) * 2
    hops = call(prepare_kernel, hop_parts, 2)(hop_x, hop_y)
    ring = length % 4 == 0 and 8 <= length <= 16 and side_x % 64 == 0
    result, residual = (by_ring if ring else by_exchange)(noise[0], phonon_level[0], hops, cosine)
    return result[None], residual[None]


def solution(mesh):
    return jax.shard_map(
        per_device,
        mesh=mesh,
        in_specs=(P(("grp", "tm"), None, None), P(("grp", "tm"), None, None), P(), P()),
        out_specs=(P(("grp", "tm"), None, None), P(("grp", "tm"), None, None)),
        check_vma=False,
    )
```
